128 devices in a mesh: tm: 8 (over y_lo, z), py: 4 (over x), pz: 4 (over y_hi, core).
Axes of the slice: x: 4, y: 4 (y_hi: 2, y_lo: 2; y = y_hi * 2 + y_lo), z: 4, core: 2. Of those that a mesh axis runs over, the one named last changes fastest.
Arguments:
- state_old: float32 [8, 4, 128, 128, 128], P('tm', None, 'py', 'pz'), may hold values from -6 to 6
Outputs:
- new_states: float32 [8, 4, 128, 128, 128], P('tm', None, 'py', 'pz')
The draws below stay inside these ranges and needn't reach their ends.
All inputs are finite; a program needn't handle non-finite values.
Results may differ from the reference program's by a relative error of at most 0.00017.
Values sent between devices are 32-bit elements; how exact they have to be, the bound alone decides.
A program may use at most 128 MiB of HBM per device.

```python
import jax
import jax.numpy as jnp
from jax import lax

N = 128
KMAX = 42
KCO = 21
SLICES = 8


def level_of(own_key, shape, split, low, top_value):
    level, own = 1.0, jax.random.fold_in(own_key, 6)
    for dim, parts in split:
        draws = jnp.exp(jax.random.uniform(jax.random.fold_in(own, dim), (parts,), jnp.float32, low / len(split), top_value / len(split)))
        level = level * jnp.repeat(draws, shape[dim] // parts).reshape([-1 if axis == dim else 1 for axis in range(len(shape))])
    return level


def normal_values(rng, dims, spread, most, shards=(), held_as=jnp.bfloat16):
    level = level_of(rng, dims, shards, -0.22, 0.18) if shards else 1.0
    entries = jax.random.normal(rng, dims, jnp.float32) * spread * level
    return jnp.minimum(jnp.maximum(entries, -most), most).astype(held_as)


def setup_inputs(seed: int = 0) -> dict:
    keys = jax.random.split(jax.random.key(seed), 2)
    state_old = normal_values(keys[0], (SLICES, 4, N, N, N), 1.0, 6.0, ((0, 8), (2, 4), (3, 4)), jnp.float32)
    return dict(state_old=state_old)


time_step = 0.01
coriolis = 6.0
buoyancy_square = 100.0
viscosity = 0.001
diffusivity = 0.001


def wave_grid():
    wave_x = jnp.arange(KMAX + 1).astype(jnp.float32)[:, None, None]
    centred = (jnp.arange(2 * KMAX + 1) - KMAX).astype(jnp.float32)
    return wave_x, centred[None, :, None], centred[None, None, :]


def synthesis(modes):
    weight = jnp.where(jnp.arange(KMAX + 1) == 0, 1.0, 2.0).astype(jnp.float32)
    weighted = modes * weight[None, :, None, None]
    padded = jnp.pad(weighted, ((0, 0), (0, N - KMAX - 1), (0, N - 2 * KMAX - 1), (0, N - 2 * KMAX - 1)))
    padded = jnp.roll(padded, (-KMAX, -KMAX), axis=(2, 3))
    return jnp.real(jnp.fft.ifftn(padded, axes=(1, 2, 3))) * (N ** 1.5)


def analysis(fields):
    spectrum = jnp.fft.fftn(fields, axes=(1, 2, 3)) * (N ** -1.5)
    rolled = jnp.roll(spectrum, (KMAX, KMAX), axis=(2, 3))
    return rolled[:, :KMAX + 1, :2 * KMAX + 1, :2 * KMAX + 1]


def project(velocity):
    wave_x, wave_y, wave_z = wave_grid()
    square = wave_x ** 2 + wave_y ** 2 + wave_z ** 2
    along = (wave_x * velocity[0] + wave_y * velocity[1] + wave_z * velocity[2]) / jnp.maximum(square, 1.0)
    return velocity[0] - wave_x * along, velocity[1] - wave_y * along, velocity[2] - wave_z * along


def rate(state):
    wave_x, wave_y, wave_z = wave_grid()
    square = wave_x ** 2 + wave_y ** 2 + wave_z ** 2
    spin = 1j * jnp.stack([wave_y * state[2] - wave_z * state[1],
                           wave_z * state[0] - wave_x * state[2],
                           wave_x * state[1] - wave_y * state[0]])
    fields = synthesis(jnp.concatenate([state, spin]))
    speed_x, speed_y, speed_z, lift = fields[0], fields[1], fields[2], fields[3]
    spin_x, spin_y, spin_z = fields[4], fields[5], fields[6]
    products = jnp.stack([speed_y * spin_z - speed_z * spin_y,
                          speed_z * spin_x - speed_x * spin_z,
                          speed_x * spin_y - speed_y * spin_x,
                          speed_x * lift, speed_y * lift, speed_z * lift])
    modes = analysis(products)
    pushed = project((modes[0] + coriolis * state[1], modes[1] - coriolis * state[0], modes[2] + state[3]))
    lift_rate = (-1j * (wave_x * modes[3] + wave_y * modes[4] + wave_z * modes[5])
                 - buoyancy_square * state[2] - diffusivity * square * state[3])
    return jnp.stack([pushed[0] - viscosity * square * state[0],
                      pushed[1] - viscosity * square * state[1],
                      pushed[2] - viscosity * square * state[2],
                      lift_rate])


def fine_step(state):
    return state + time_step * rate(state)


def linear(state):
    wave_x, wave_y, wave_z = wave_grid()
    square = wave_x ** 2 + wave_y ** 2 + wave_z ** 2
    pushed = project((coriolis * state[1], -coriolis * state[0], state[3]))
    return jnp.stack([pushed[0] - viscosity * square * state[0],
                      pushed[1] - viscosity * square * state[1],
                      pushed[2] - viscosity * square * state[2],
                      -buoyancy_square * state[2] - diffusivity * square * state[3]])


def propagate(state):
    for half_step in range(2):
        anchor = state
        for order in (4.0, 3.0, 2.0, 1.0):
            state = anchor + (0.5 * time_step / order) * linear(state)
    return state


def reference(state_old):
    def one_slice(fields):
        physical = jnp.transpose(fields, (0, 3, 1, 2))
        start = analysis(physical)
        velocity = project((start[0], start[1], start[2]))
        start = jnp.concatenate([jnp.stack(velocity), start[3:]])
        return start, fine_step(start)

    starts, fines = lax.map(one_slice, state_old)
    wave_x, wave_y, wave_z = wave_grid()
    inside = (wave_x <= KCO) & (jnp.abs(wave_y) <= KCO) & (jnp.abs(wave_z) <= KCO)
    keep = inside.astype(jnp.float32)
    outputs = []
    carry = keep * fines[0]
    for index in range(SLICES):
        if index > 0:
            carry = keep * fines[index] - keep * propagate(starts[index]) + keep * propagate(carry)
        merged = jnp.where(inside, carry, fines[index])
        outputs.append(jnp.transpose(synthesis(merged), (0, 2, 3, 1)))
    return jnp.stack(outputs)
```

```python
import functools

import jax
import jax.numpy as jnp
import numpy as np
from jax import lax
from jax.experimental import pallas as pl
from jax.experimental.pallas import tpu as pltpu
from jax.sharding import PartitionSpec as P

KMAX = 42
KCO = 21
N = 128
KY = 96
PLANES = 3
GROUP = 16
BLOCK = 32
MODE_ROWS = 2 * PLANES * GROUP
SCAN = 6
MESH = pl.DeviceIdType.MESH
VMEM_BYTES = 50 << 20

time_step = 0.01
coriolis = 6.0
buoyancy_square = 100.0
viscosity = 0.001
diffusivity = 0.001


def halves(table):
    exact = jnp.asarray(table, jnp.float32)
    high = exact.astype(jnp.bfloat16)
    low = (exact - high.astype(jnp.float32)).astype(jnp.bfloat16)
    return high, low


def tables():
    scale = N**-0.5
    cells = np.arange(N)
    waves_x = np.arange(GROUP)[:, None] + GROUP * np.arange(PLANES)[None, :]
    angle = 2 * np.pi / N * ((waves_x[:, :, None] * cells) % N)
    inside = (waves_x <= KMAX)[:, :, None] * scale
    fore = np.stack([np.cos(angle), -np.sin(angle)], axis=2) * inside[:, :, None]
    weight = np.where(waves_x == 0, 1.0, 2.0)[:, :, None, None]
    back = fore * weight
    rest = ((0, N - MODE_ROWS), (0, 0))
    fore = np.pad(fore.reshape(MODE_ROWS, N), rest).T
    back = np.pad(back.reshape(MODE_ROWS, N), rest)

    def one_pass(table):
        high, low = halves(table)
        return jnp.concatenate(
            [
                jnp.concatenate([high, low], axis=1),
                jnp.concatenate([high, jnp.zeros_like(high)], axis=1),
            ]
        )

    def pair(slots):
        waves = np.arange(slots) - KMAX
        angle = 2 * np.pi / N * ((waves[:, None] * cells[None, :]) % N)
        inside = (waves <= KMAX)[:, None] * scale
        return np.cos(angle) * inside, np.sin(angle) * inside

    cos_y, sin_y = pair(KY)
    cos_z, sin_z = pair(N)
    fore_y = np.block([[cos_y, sin_y], [-sin_y, cos_y]])
    back_y = np.block([[cos_y.T, -sin_y.T], [sin_y.T, cos_y.T]])
    fore_z = np.block([[cos_z.T, -sin_z.T], [sin_z.T, cos_z.T]])
    back_z = np.block([[cos_z, sin_z], [-sin_z, cos_z]])
    stack = lambda table: jnp.concatenate(halves(table))
    return dict(
        fore_x=one_pass(fore),
        back_x=one_pass(back),
        fore_y=stack(fore_y),
        back_y=stack(back_y),
        fore_z=stack(fore_z),
        back_z=stack(back_z),
    )


def split(values):
    high = values.astype(jnp.bfloat16)
    low = (values - high.astype(jnp.float32)).astype(jnp.bfloat16)
    return high, low


def mul(left, right):
    return jnp.dot(left, right, preferred_element_type=jnp.float32)


def by_x(values, table):
    out = mul(jnp.concatenate(split(values), axis=1), table[...])
    return out[:, :N] + out[:, N:]


def by_left(table, values):
    rows = table.shape[0] // 2
    high, low = split(values)
    out = mul(table[...], high)
    return out[:rows] + out[rows:] + mul(table[:rows], low)


def by_right(values, table):
    rows = table.shape[0] // 2
    high, low = split(values)
    return mul(high, table[:rows]) + mul(low, table[:rows]) + mul(high, table[rows:])


def swap_groups(parts):
    lane = lax.broadcasted_iota(jnp.int32, parts[0].shape, 1)
    low_half = lane < 64
    even = (lane // 32) % 2 == 0
    a0, a1, a2, a3 = parts
    p0 = jnp.where(low_half, a0, pltpu.roll(a2, 64, 1))
    p2 = jnp.where(low_half, pltpu.roll(a0, 64, 1), a2)
    p1 = jnp.where(low_half, a1, pltpu.roll(a3, 64, 1))
    p3 = jnp.where(low_half, pltpu.roll(a1, 64, 1), a3)
    return (
        jnp.where(even, p0, pltpu.roll(p1, 32, 1)),
        jnp.where(even, pltpu.roll(p0, 96, 1), p1),
        jnp.where(even, p2, pltpu.roll(p3, 32, 1)),
        jnp.where(even, pltpu.roll(p2, 96, 1), p3),
    )


def place():
    tm, py, pz = lax.axis_index("tm"), lax.axis_index("py"), lax.axis_index("pz")
    return tm, py, pz, py * 4 + pz


def meet_group(barrier):
    tm, py, pz, _ = place()

    def greet(i, carry):
        peer = (tm, (py + i // 4) % 4, (pz + i % 4) % 4)
        pl.semaphore_signal(barrier, inc=1, device_id=peer, device_id_type=MESH)
        return carry

    lax.fori_loop(1, GROUP, greet, 0)


def chunk(owner, plane):
    rows = 2 * BLOCK
    start = pl.multiple_of((owner * PLANES + plane) * rows, rows)
    return pl.ds(start, rows)


class Exchange:
    def __init__(self, source, target, send, receive, own):
        self.source, self.target = source, target
        self.send, self.receive, self.own = send, receive, own

    def local(self, plane):
        _, _, _, me = place()
        part = chunk(me, plane)
        return pltpu.make_async_copy(
            self.source.at[part, :], self.target.at[part, :], self.own.at[plane]
        )

    def remote(self, i, plane, origin):
        tm, py, pz, me = place()
        to_y, to_z = (py + i // 4) % 4, (pz + i % 4) % 4
        from_y, from_z = (py + 4 - i // 4) % 4, (pz + 4 - i % 4) % 4
        where = (from_y * 4 + from_z) if origin else me
        index = plane * GROUP + i
        return pltpu.make_async_remote_copy(
            src_ref=self.source.at[chunk(to_y * 4 + to_z, plane), :],
            dst_ref=self.target.at[chunk(where, plane), :],
            send_sem=self.send.at[index],
            recv_sem=self.receive.at[index],
            device_id=(tm, to_y, to_z),
            device_id_type=MESH,
        )

    def start(self, plane):
        def go(i, carry):
            self.remote(i, plane, False).start()
            return carry

        lax.fori_loop(1, GROUP, go, 0)
        self.local(plane).start()

    def arrived(self, plane):
        def go(i, carry):
            self.remote(i, plane, True).wait_recv()
            return carry

        lax.fori_loop(1, GROUP, go, 0)
        self.local(plane).wait()

    def sent(self, plane):
        def go(i, carry):
            self.remote(i, plane, False).wait_send()
            return carry

        lax.fori_loop(1, GROUP, go, 0)


def exchange_scratch():
    return [
        pltpu.VMEM((MODE_ROWS * BLOCK, N), jnp.float32),
        pltpu.VMEM((MODE_ROWS * BLOCK, N), jnp.float32),
        pltpu.SemaphoreType.DMA((PLANES * GROUP,)),
        pltpu.SemaphoreType.DMA((PLANES * GROUP,)),
        pltpu.SemaphoreType.DMA((PLANES,)),
    ]


def store_modes_x(fields, table, target, first, count):
    modes = by_x(fields, table)
    for y in range(count):
        turned = modes[y * N : (y + 1) * N].T
        target[pl.ds(first + y, MODE_ROWS, stride=BLOCK), :] = turned[:MODE_ROWS]


def load_fields_x(source, table, first, count):
    lines = []
    for y in range(count):
        rows = source[pl.ds(first + y, MODE_ROWS, stride=BLOCK), :]
        rows = jnp.concatenate([rows, jnp.zeros((N - MODE_ROWS, N), jnp.float32)])
        lines.append(rows.T)
    return by_x(jnp.concatenate(lines), table)


def fore_plane(received, plane, planes, fore_y, fore_z):
    for part in range(2):
        for block in range(4):
            blocks = []
            for s in range(4):
                start = (((block * 4 + s) * PLANES + plane) * 2 + part) * BLOCK
                blocks.append(received[pl.ds(pl.multiple_of(start, BLOCK), BLOCK), :])
            for f, piece in enumerate(swap_groups(blocks)):
                rows = pl.ds(part * N + block * BLOCK, BLOCK)
                planes[f // 2, rows, (f % 2) * N : (f % 2 + 1) * N] = piece
    lines = []
    for duo in range(2):
        along_y = by_left(fore_y, planes[duo])
        for f in range(2):
            own = along_y[:, f * N : (f + 1) * N]
            lines.append(jnp.concatenate([own[:KY], own[KY:]], axis=1))
    return by_right(jnp.concatenate(lines), fore_z)


def back_plane(modes, plane, target, back_y, back_z):
    along_z = by_right(modes, back_z)
    fields = []
    for duo in range(2):
        both = []
        for f in range(2):
            own = along_z[(2 * duo + f) * KY : (2 * duo + f + 1) * KY]
            both.append(jnp.concatenate([own[:, :N], own[:, N:]]))
        along_y = by_left(back_y, jnp.concatenate(both, axis=1))
        fields += [along_y[:, :N], along_y[:, N:]]
    for part in range(2):
        for block in range(4):
            rows = slice(part * N + block * BLOCK, part * N + (block + 1) * BLOCK)
            for s, piece in enumerate(swap_groups([field[rows] for field in fields])):
                start = (((block * 4 + s) * PLANES + plane) * 2 + part) * BLOCK
                target[pl.ds(pl.multiple_of(start, BLOCK), BLOCK), :] = piece


def waves_at(plane):
    _, _, _, me = place()
    wave_x = (me + GROUP * plane).astype(jnp.float32)
    wave_y = (lax.broadcasted_iota(jnp.int32, (KY, N), 0) - KMAX).astype(jnp.float32)
    wave_z = (lax.broadcasted_iota(jnp.int32, (KY, N), 1) - KMAX).astype(jnp.float32)
    return wave_x, wave_y, wave_z


def squared(waves):
    wave_x, wave_y, wave_z = waves
    return wave_x * wave_x + wave_y * wave_y + wave_z * wave_z


def project(velocity, waves, inverse):
    wave_x, wave_y, wave_z = waves
    along = (wave_x * velocity[0] + wave_y * velocity[1] + wave_z * velocity[2]) * inverse
    return (
        velocity[0] - wave_x * along,
        velocity[1] - wave_y * along,
        velocity[2] - wave_z * along,
    )


def linear(state, waves, square, inverse):
    pushed = project((coriolis * state[1], -coriolis * state[0], state[3]), waves, inverse)
    return (
        pushed[0] - viscosity * square * state[0],
        pushed[1] - viscosity * square * state[1],
        pushed[2] - viscosity * square * state[2],
        -buoyancy_square * state[2] - diffusivity * square * state[3],
    )


def propagate(state, waves):
    square = squared(waves)
    inverse = 1.0 / jnp.maximum(square, 1.0)
    for half_step in range(2):
        anchor = state
        for order in (4.0, 3.0, 2.0, 1.0):
            rate = linear(state, waves, square, inverse)
            state = tuple(a + (0.5 * time_step / order) * r for a, r in zip(anchor, rate))
    return state


def analysis_kernel(
    fields, fore_x, fore_y, fore_z, start, out, into, send, receive, own, planes
):
    barrier = pltpu.get_barrier_semaphore()
    meet_group(barrier)

    def lines(step, carry):
        first = step * 4
        block = fields[:, pl.ds(first, 4)]
        rows = [block[f, y] for y in range(4) for f in range(4)]
        store_modes_x(jnp.concatenate(rows), fore_x, out, first, 4)
        return carry

    lax.fori_loop(0, BLOCK // 4, lines, 0)
    pl.semaphore_wait(barrier, GROUP - 1)
    exchange = Exchange(out, into, send, receive, own)
    for plane in range(PLANES):
        exchange.start(plane)

    def finish(plane, carry):
        exchange.arrived(plane)
        modes = fore_plane(into, plane, planes, fore_y, fore_z)
        waves = waves_at(plane)
        inverse = 1.0 / jnp.maximum(squared(waves), 1.0)
        for part in range(2):
            own_lanes = slice(part * N, (part + 1) * N)
            state = [modes[f * KY : (f + 1) * KY, own_lanes] for f in range(4)]
            for f, value in enumerate(project(state[:3], waves, inverse) + (state[3],)):
                start[plane, pl.ds(f * KY, KY), own_lanes] = value
        exchange.sent(plane)
        return carry

    lax.fori_loop(0, PLANES, finish, 0)


def rate_kernel(
    start, fore_x, back_x, fore_y, back_y, fore_z, back_z, fine,
    out0, into0, send0, receive0, own0,
    out1, into1, send1, receive1, own1,
    out2, into2, send2, receive2, own2,
    planes, first_modes, second_modes,
):
    barrier = pltpu.get_barrier_semaphore()
    meet_group(barrier)
    to_grid = Exchange(out0, into0, send0, receive0, own0)
    to_modes = (
        Exchange(out1, into1, send1, receive1, own1),
        Exchange(out2, into2, send2, receive2, own2),
    )
    back_plane(start[0], 0, out0, back_y, back_z)
    pl.semaphore_wait(barrier, GROUP - 1)
    to_grid.start(0)

    def spread(plane, carry):
        back_plane(start[plane], plane, out0, back_y, back_z)
        to_grid.start(plane)
        return carry

    lax.fori_loop(1, PLANES, spread, 0)

    def gather(plane, carry):
        to_grid.arrived(plane)
        return carry

    lax.fori_loop(0, PLANES, gather, 0)

    def lines(step, carry):
        first = step * 4
        grid = load_fields_x(into0, back_x, first, 4)
        one, two = [], []
        for y in range(4):
            u, v, w, b = (
                grid[y * N + f * BLOCK : y * N + (f + 1) * BLOCK] for f in range(4)
            )
            rest = w * w
            one += [u * u - rest, v * v - rest, u * v, u * w]
            two += [v * w, u * b, v * b, w * b]
        store_modes_x(jnp.concatenate(one), fore_x, out1, first, 4)
        store_modes_x(jnp.concatenate(two), fore_x, out2, first, 4)
        return carry

    lax.fori_loop(0, BLOCK // 4, lines, 0)
    for plane in range(PLANES):
        for exchange in to_modes:
            exchange.start(plane)

    def finish(plane, carry):
        to_modes[0].arrived(plane)
        first_modes[...] = fore_plane(into1, plane, planes, fore_y, fore_z)
        to_modes[1].arrived(plane)
        second_modes[...] = fore_plane(into2, plane, planes, fore_y, fore_z)
        waves = waves_at(plane)
        wave_x, wave_y, wave_z = waves
        square = squared(waves)
        inverse = 1.0 / jnp.maximum(square, 1.0)

        def products(lanes):
            return [first_modes[f * KY : (f + 1) * KY, lanes] for f in range(4)] + [
                second_modes[f * KY : (f + 1) * KY, lanes] for f in range(4)
            ]

        for part in range(2):
            lanes = slice(part * N, (part + 1) * N)
            other = slice((1 - part) * N, (2 - part) * N)
            sign = 1.0 if part == 0 else -1.0
            xx, yy, xy, xz, yz, bx, by, bz = products(other)
            state = [start[plane, pl.ds(f * KY, KY), lanes] for f in range(4)]
            moved = (
                sign * (wave_x * xx + wave_y * xy + wave_z * xz),
                sign * (wave_x * xy + wave_y * yy + wave_z * yz),
                sign * (wave_x * xz + wave_y * yz),
            )
            lifted = sign * (wave_x * bx + wave_y * by + wave_z * bz)
            pushed = project(
                (
                    moved[0] + coriolis * state[1],
                    moved[1] - coriolis * state[0],
                    moved[2] + state[3],
                ),
                waves,
                inverse,
            )
            rates = [pushed[f] - viscosity * square * state[f] for f in range(3)]
            rates.append(
                lifted - buoyancy_square * state[2] - diffusivity * square * state[3]
            )
            for f in range(4):
                fine[plane, pl.ds(f * KY, KY), lanes] = state[f] + time_step * rates[f]
        to_grid.sent(plane)
        for exchange in to_modes:
            exchange.sent(plane)
        return carry

    lax.fori_loop(0, PLANES, finish, 0)


FIRST_ROW = 16
COARSE_ROWS = 8 * SCAN
TILE = 8 * 4 * 2


def coarse_waves(plane, row0, rows):
    _, _, _, me = place()
    row = lax.broadcasted_iota(jnp.int32, (rows, N), 0) + row0
    lane = lax.broadcasted_iota(jnp.int32, (rows, N), 1) % 64
    wave_x = (me + GROUP * plane).astype(jnp.float32)
    wave_y = (row - KMAX).astype(jnp.float32)
    wave_z = (lane - KMAX).astype(jnp.float32)
    return wave_x, wave_y, wave_z


def coarse_inside(waves):
    wave_x, wave_y, wave_z = waves
    inside = (jnp.abs(wave_y) <= KCO) & (jnp.abs(wave_z) <= KCO)
    return inside & jnp.broadcast_to(wave_x <= KCO, inside.shape)


def packed(ref, plane, f):
    rows = pl.ds(f * KY + FIRST_ROW, COARSE_ROWS)
    lane = lax.broadcasted_iota(jnp.int32, (COARSE_ROWS, N), 1)
    real, imag = ref[plane, rows, :N], ref[plane, rows, N:]
    return jnp.where(lane < 64, real, pltpu.roll(imag, 64, 1))


def last_kernel(
    fine, start, back_x, back_y, back_z, result,
    out, into, send, receive, own, merged,
    coarse_out, coarse_in, coarse_send, coarse_receive, coarse_own,
    carry_out, carry_in, carry_send, carry_receive, carry_own,
):
    tm, py, pz, me = place()
    slices = lax.axis_size("tm")
    barrier = pltpu.get_barrier_semaphore()
    meet_group(barrier)

    def greet(i, carry):
        peer = ((tm + i) % slices, py, pz)
        pl.semaphore_signal(barrier, inc=1, device_id=peer, device_id_type=MESH)
        return carry

    lax.fori_loop(1, slices, greet, 0)

    def rows_of(index):
        return pl.ds(pl.multiple_of(index * TILE, TILE), TILE)

    def coarse_copy(i, origin):
        to = (tm + i) % slices
        where = (tm + slices - i) % slices if origin else tm
        return pltpu.make_async_remote_copy(
            src_ref=coarse_out.at[rows_of(to), :],
            dst_ref=coarse_in.at[rows_of(where), :],
            send_sem=coarse_send.at[i],
            recv_sem=coarse_receive.at[i],
            device_id=(to, py, pz),
            device_id_type=MESH,
        )

    def carry_copy(i, origin):
        to = (tm + i) % slices
        where = (tm + slices - i) % slices if origin else tm
        return pltpu.make_async_remote_copy(
            src_ref=carry_out.at[rows_of(to), :],
            dst_ref=carry_in.at[rows_of(where), :],
            send_sem=carry_send.at[i],
            recv_sem=carry_receive.at[i],
            device_id=(to, py, pz),
            device_id_type=MESH,
        )

    coarse_mine = pltpu.make_async_copy(
        coarse_out.at[rows_of(tm), :], coarse_in.at[rows_of(tm), :], coarse_own
    )
    carry_mine = pltpu.make_async_copy(
        carry_out.at[rows_of(tm), :], carry_in.at[rows_of(tm), :], carry_own
    )

    for plane in range(2):
        waves = coarse_waves(plane, FIRST_ROW, COARSE_ROWS)
        keep = coarse_inside(waves).astype(jnp.float32)
        before = [packed(start, plane, f) for f in range(4)]
        after = [packed(fine, plane, f) for f in range(4)]
        moved = propagate(tuple(before), waves)
        for f in range(4):
            here = keep * after[f] - jnp.where(tm > 0, keep * moved[f], 0.0)
            for tile in range(SCAN):
                place_at = tile * TILE + (f * 2 + plane) * 8
                coarse_out[place_at : place_at + 8, :] = here[tile * 8 : tile * 8 + 8]

    pl.semaphore_wait(barrier, GROUP - 1 + slices - 1)

    def coarse_go(i, carry):
        @pl.when((tm + i) % slices < SCAN)
        def _():
            coarse_copy(i, False).start()

        return carry

    lax.fori_loop(1, slices, coarse_go, 0)

    @pl.when(tm < SCAN)
    def _():
        coarse_mine.start()

    exchange = Exchange(out, into, send, receive, own)
    back_plane(fine[2], 2, out, back_y, back_z)
    exchange.start(2)

    @pl.when(tm < SCAN)
    def _():
        def wait(i, carry):
            coarse_copy(i, True).wait_recv()
            return carry

        lax.fori_loop(1, slices, wait, 0)
        coarse_mine.wait()
        row0 = FIRST_ROW + tm * 8
        waves = [coarse_waves(plane, row0, 8) for plane in range(2)]
        keep = [coarse_inside(w).astype(jnp.float32) for w in waves]

        def step(n, state):
            base = pl.multiple_of(n * TILE, TILE)
            new = []
            for plane in range(2):
                moved = propagate(tuple(state[plane * 4 : plane * 4 + 4]), waves[plane])
                for f in range(4):
                    rows = pl.ds(base + (f * 2 + plane) * 8, 8)
                    value = coarse_in[rows, :] + keep[plane] * moved[f]
                    carry_out[rows, :] = value
                    new.append(value)
            return tuple(new)

        lax.fori_loop(0, slices, step, tuple([jnp.zeros((8, N), jnp.float32)] * 8))

        def back(i, carry):
            carry_copy(i, False).start()
            return carry

        lax.fori_loop(1, slices, back, 0)
        carry_mine.start()

    def carry_wait(i, carry):
        @pl.when((tm + slices - i) % slices < SCAN)
        def _():
            carry_copy(i, True).wait_recv()

        return carry

    lax.fori_loop(1, slices, carry_wait, 0)

    @pl.when(tm < SCAN)
    def _():
        carry_mine.wait()

    for plane in range(2):
        waves = coarse_waves(plane, FIRST_ROW, COARSE_ROWS)
        inside = coarse_inside(waves)
        lane = lax.broadcasted_iota(jnp.int32, (COARSE_ROWS, N), 1)
        here = inside & (lane < 64)
        merged[...] = fine[plane]
        for f in range(4):
            tiles = []
            for tile in range(SCAN):
                place_at = tile * TILE + (f * 2 + plane) * 8
                tiles.append(carry_in[place_at : place_at + 8, :])
            value = jnp.concatenate(tiles)
            rows = pl.ds(f * KY + FIRST_ROW, COARSE_ROWS)
            merged[rows, :N] = jnp.where(here, value, merged[rows, :N])
            merged[rows, N:] = jnp.where(here, pltpu.roll(value, 64, 1), merged[rows, N:])
        back_plane(merged[...], plane, out, back_y, back_z)
        exchange.start(plane)

    def gather(plane, carry):
        exchange.arrived(plane)
        return carry

    lax.fori_loop(0, PLANES, gather, 0)

    def lines(step, carry):
        first = step * 4
        grid = load_fields_x(into, back_x, first, 4)
        for y in range(4):
            for f in range(4):
                at = y * N + f * BLOCK
                result[f, first + y] = grid[at : at + BLOCK]
        return carry

    lax.fori_loop(0, BLOCK // 4, lines, 0)

    def done(plane, carry):
        exchange.sent(plane)
        return carry

    lax.fori_loop(0, PLANES, done, 0)

    def coarse_done(i, carry):
        @pl.when((tm + i) % slices < SCAN)
        def _():
            coarse_copy(i, False).wait_send()

        @pl.when(tm < SCAN)
        def _():
            carry_copy(i, False).wait_send()

        return carry

    lax.fori_loop(1, slices, coarse_done, 0)

    @pl.when(tm < SCAN)
    def _():
        pass


def call(kernel, name, out, scratch, collective, *args):
    return pl.pallas_call(
        kernel,
        name=name,
        out_shape=jax.ShapeDtypeStruct(out, jnp.float32),
        in_specs=[pl.BlockSpec(memory_space=pltpu.VMEM)] * len(args),
        out_specs=pl.BlockSpec(memory_space=pltpu.VMEM),
        scratch_shapes=scratch,
        compiler_params=pltpu.CompilerParams(
            collective_id=collective, has_side_effects=True, vmem_limit_bytes=VMEM_BYTES
        ),
    )(*args)


def on_device(state_old):
    t = tables()
    slices = lax.axis_size("tm")
    modes_shape = (PLANES, 4 * KY, 2 * N)
    planes = pltpu.VMEM((2, 2 * N, 2 * N), jnp.float32)
    start = call(
        analysis_kernel,
        "analysis",
        modes_shape,
        exchange_scratch() + [planes],
        0,
        state_old[0],
        t["fore_x"],
        t["fore_y"],
        t["fore_z"],
    )
    half = pltpu.VMEM((4 * KY, 2 * N), jnp.float32)
    fine = call(
        rate_kernel,
        "rate",
        modes_shape,
        exchange_scratch() * 3 + [planes, half, half],
        1,
        start,
        t["fore_x"],
        t["back_x"],
        t["fore_y"],
        t["back_y"],
        t["fore_z"],
        t["back_z"],
    )
    passes = [
        pltpu.VMEM((slices * TILE, N), jnp.float32),
        pltpu.VMEM((slices * TILE, N), jnp.float32),
        pltpu.SemaphoreType.DMA((slices,)),
        pltpu.SemaphoreType.DMA((slices,)),
        pltpu.SemaphoreType.DMA,
    ]
    result = call(
        last_kernel,
        "last",
        state_old.shape[1:],
        exchange_scratch() + [half] + passes + passes,
        2,
        fine,
        start,
        t["back_x"],
        t["back_y"],
        t["back_z"],
    )
    return result[None]


def solution(mesh):
    return jax.shard_map(
        on_device,
        mesh=mesh,
        in_specs=(P("tm", None, "py", "pz", None),),
        out_specs=P("tm", None, "py", "pz", None),
        check_vma=False,
    )
```

```python
import functools

import jax
import jax.numpy as jnp
import numpy as np
from jax import lax
from jax.experimental import pallas as pl
from jax.experimental.pallas import tpu as pltpu
from jax.sharding import PartitionSpec as P

KMAX = 42
KCO = 21
N = 128
KY = 96
PLANES = 3
GROUP = 16
BLOCK = 32
MODE_ROWS = 88
HOLDERS = KMAX + 1 - 2 * GROUP
GRID_ROWS = MODE_ROWS * BLOCK
PLANE_ROWS = PLANES * GROUP * 2 * BLOCK
SCAN = 6
MESH = pl.DeviceIdType.MESH
VMEM_BYTES = 50 << 20

time_step = 0.01
coriolis = 6.0
buoyancy_square = 100.0
viscosity = 0.001
diffusivity = 0.001


def halves(table):
    exact = np.asarray(table, np.float32)
    high = exact.astype(jnp.bfloat16)
    low = (exact - high.astype(np.float32)).astype(jnp.bfloat16)
    return high, low


def tables():
    scale = N**-0.5
    cells = np.arange(N)
    waves_x = np.arange(PLANES * GROUP)
    angle = 2 * np.pi / N * ((waves_x[:, None] * cells) % N)
    inside = (waves_x <= KMAX)[:, None] * scale
    fore = np.stack([np.cos(angle), -np.sin(angle)], axis=1) * inside[:, None]
    weight = np.where(waves_x == 0, 1.0, 2.0)[:, None, None]
    back = fore * weight
    rest = ((0, N - 2 * PLANES * GROUP), (0, 0))
    fore = np.pad(fore.reshape(-1, N), rest).T
    back = np.pad(back.reshape(-1, N), rest)

    def one_pass(table):
        high, low = halves(table)
        return np.concatenate(
            [
                np.concatenate([high, low], axis=1),
                np.concatenate([high, np.zeros_like(high)], axis=1),
            ]
        )

    def pair(slots):
        waves = np.arange(slots) - KMAX
        angle = 2 * np.pi / N * ((waves[:, None] * cells[None, :]) % N)
        inside = (waves <= KMAX)[:, None] * scale
        return np.cos(angle) * inside, np.sin(angle) * inside

    cos_y, sin_y = pair(KY)
    cos_z, sin_z = pair(N)
    fore_y = np.block([[cos_y, sin_y], [-sin_y, cos_y]])
    back_y = np.block([[cos_y.T, -sin_y.T], [sin_y.T, cos_y.T]])
    fore_z = np.block([[cos_z.T, -sin_z.T], [sin_z.T, cos_z.T]])
    back_z = np.block([[cos_z, sin_z], [-sin_z, cos_z]])
    stack = lambda table: np.concatenate(halves(table))
    return (
        one_pass(fore),
        one_pass(back),
        stack(fore_y),
        stack(back_y),
        stack(fore_z),
        stack(back_z),
    )


def split(values):
    high = values.astype(jnp.bfloat16)
    low = (values - high.astype(jnp.float32)).astype(jnp.bfloat16)
    return high, low


def mul(left, right):
    return jnp.dot(left, right, preferred_element_type=jnp.float32)


def by_x(values, table):
    out = mul(jnp.concatenate(split(values), axis=1), table[...])
    return out[:, :N] + out[:, N:]


def by_left(table, values):
    rows = table.shape[0] // 2
    high, low = split(values)
    out = mul(table[...], high)
    return out[:rows] + out[rows:] + mul(table[:rows], low)


def by_right(values, table):
    rows = table.shape[0] // 2
    high, low = split(values)
    return mul(high, table[:rows]) + mul(low, table[:rows]) + mul(high, table[rows:])


def swap_groups(parts):
    lane = lax.broadcasted_iota(jnp.int32, parts[0].shape, 1)
    low_half = lane < 64
    even = (lane // 32) % 2 == 0
    a0, a1, a2, a3 = parts
    p0 = jnp.where(low_half, a0, pltpu.roll(a2, 64, 1))
    p2 = jnp.where(low_half, pltpu.roll(a0, 64, 1), a2)
    p1 = jnp.where(low_half, a1, pltpu.roll(a3, 64, 1))
    p3 = jnp.where(low_half, pltpu.roll(a1, 64, 1), a3)
    return (
        jnp.where(even, p0, pltpu.roll(p1, 32, 1)),
        jnp.where(even, pltpu.roll(p0, 96, 1), p1),
        jnp.where(even, p2, pltpu.roll(p3, 32, 1)),
        jnp.where(even, pltpu.roll(p2, 96, 1), p3),
    )


def place():
    tm, py, pz = lax.axis_index("tm"), lax.axis_index("py"), lax.axis_index("pz")
    return tm, py, pz, py * 4 + pz


def chunk(owner, plane):
    rows = 2 * BLOCK
    return pl.ds(pl.multiple_of((plane * GROUP + owner) * rows, rows), rows)


class Exchange:
    def __init__(self, refs, to_modes):
        self.source, self.target, self.send, self.receive, self.own = refs
        self.to_modes = to_modes

    def local(self, plane):
        _, _, _, me = place()
        part = chunk(me, plane)
        return pltpu.make_async_copy(
            self.source.at[part, :], self.target.at[part, :], self.own.at[plane]
        )

    def remote(self, i, plane):
        tm, py, pz, me = place()
        to_y, to_z = (py + i // 4) % 4, (pz + i % 4) % 4
        return pltpu.make_async_remote_copy(
            src_ref=self.source.at[chunk(to_y * 4 + to_z, plane), :],
            dst_ref=self.target.at[chunk(me, plane), :],
            send_sem=self.send.at[plane],
            recv_sem=self.receive.at[plane],
            device_id=(tm, to_y, to_z),
            device_id_type=MESH,
        )

    def amount(self, count, plane):
        tm, py, pz, _ = place()
        rows = pl.ds(0, count * 2 * BLOCK)
        return pltpu.make_async_remote_copy(
            src_ref=self.source.at[rows, :],
            dst_ref=self.target.at[rows, :],
            send_sem=self.send.at[plane],
            recv_sem=self.receive.at[plane],
            device_id=(tm, (py + 1) % 4, pz),
            device_id_type=MESH,
        )

    def start(self, plane):
        _, py, pz, me = place()

        def go(i, carry):
            to = (py + i // 4) % 4 * 4 + (pz + i % 4) % 4
            wanted = (to if self.to_modes else me) + GROUP * plane <= KMAX

            @pl.when(wanted)
            def _():
                self.remote(i, plane).start()

            return carry

        lax.fori_loop(1, GROUP, go, 0)

        @pl.when(me + GROUP * plane <= KMAX)
        def _():
            self.local(plane).start()

    def modes_side(self, plane, done):
        _, _, _, me = place()

        @pl.when(me + GROUP * plane <= KMAX)
        def _():
            done(self.amount(GROUP - 1, plane))

    def grid_side(self, plane, done):
        _, _, _, me = place()

        @pl.when(plane < PLANES - 1)
        def _():
            done(self.amount(GROUP - 1, plane))

        @pl.when((plane == PLANES - 1) & (me < HOLDERS))
        def _():
            done(self.amount(HOLDERS - 1, plane))

        @pl.when((plane == PLANES - 1) & (me >= HOLDERS))
        def _():
            done(self.amount(HOLDERS, plane))

    def arrived(self, plane):
        _, _, _, me = place()
        side = self.modes_side if self.to_modes else self.grid_side
        side(plane, lambda copy: copy.wait_recv())

        @pl.when(me + GROUP * plane <= KMAX)
        def _():
            self.local(plane).wait()

    def sent(self, plane):
        side = self.grid_side if self.to_modes else self.modes_side
        side(plane, lambda copy: copy.wait_send())


def exchange_scratch(to_modes):
    sizes = (GRID_ROWS, PLANE_ROWS)
    source, target = sizes if to_modes else sizes[::-1]
    return [
        pltpu.VMEM((source, N), jnp.float32),
        pltpu.VMEM((target, N), jnp.float32),
        pltpu.SemaphoreType.DMA((PLANES,)),
        pltpu.SemaphoreType.DMA((PLANES,)),
        pltpu.SemaphoreType.DMA((PLANES,)),
    ]


def store_modes_x(fields, table, target, first, count):
    modes = by_x(fields, table)
    for y in range(count):
        turned = modes[y * N : (y + 1) * N].T
        target[pl.ds(first + y, MODE_ROWS, stride=BLOCK), :] = turned[:MODE_ROWS]


def load_fields_x(source, table, first, count):
    lines = []
    for y in range(count):
        rows = source[pl.ds(first + y, MODE_ROWS, stride=BLOCK), :]
        rows = jnp.concatenate([rows, jnp.zeros((N - MODE_ROWS, N), jnp.float32)])
        lines.append(rows.T)
    return by_x(jnp.concatenate(lines), table)


def fore_plane(received, plane, planes, fore_y, fore_z):
    for part in range(2):
        for block in range(4):
            blocks = []
            for s in range(4):
                start = ((plane * GROUP + block * 4 + s) * 2 + part) * BLOCK
                blocks.append(received[pl.ds(pl.multiple_of(start, BLOCK), BLOCK), :])
            for f, piece in enumerate(swap_groups(blocks)):
                rows = pl.ds(part * N + block * BLOCK, BLOCK)
                planes[f // 2, rows, (f % 2) * N : (f % 2 + 1) * N] = piece
    lines = []
    for duo in range(2):
        along_y = by_left(fore_y, planes[duo])
        for f in range(2):
            own = along_y[:, f * N : (f + 1) * N]
            lines.append(jnp.concatenate([own[:KY], own[KY:]], axis=1))
    return by_right(jnp.concatenate(lines), fore_z)


def back_plane(modes, plane, target, back_y, back_z):
    along_z = by_right(modes, back_z)
    fields = []
    for duo in range(2):
        both = []
        for f in range(2):
            own = along_z[(2 * duo + f) * KY : (2 * duo + f + 1) * KY]
            both.append(jnp.concatenate([own[:, :N], own[:, N:]]))
        along_y = by_left(back_y, jnp.concatenate(both, axis=1))
        fields += [along_y[:, :N], along_y[:, N:]]
    for part in range(2):
        for block in range(4):
            rows = slice(part * N + block * BLOCK, part * N + (block + 1) * BLOCK)
            for s, piece in enumerate(swap_groups([field[rows] for field in fields])):
                start = ((plane * GROUP + block * 4 + s) * 2 + part) * BLOCK
                target[pl.ds(pl.multiple_of(start, BLOCK), BLOCK), :] = piece


def waves_at(plane):
    _, _, _, me = place()
    wave_x = (me + GROUP * plane).astype(jnp.float32)
    wave_y = (lax.broadcasted_iota(jnp.int32, (KY, N), 0) - KMAX).astype(jnp.float32)
    wave_z = (lax.broadcasted_iota(jnp.int32, (KY, N), 1) - KMAX).astype(jnp.float32)
    return wave_x, wave_y, wave_z


def squared(waves):
    wave_x, wave_y, wave_z = waves
    return wave_x * wave_x + wave_y * wave_y + wave_z * wave_z


def project(velocity, waves, inverse):
    wave_x, wave_y, wave_z = waves
    along = (wave_x * velocity[0] + wave_y * velocity[1] + wave_z * velocity[2]) * inverse
    return (
        velocity[0] - wave_x * along,
        velocity[1] - wave_y * along,
        velocity[2] - wave_z * along,
    )


def linear(state, waves, square, inverse):
    pushed = project((coriolis * state[1], -coriolis * state[0], state[3]), waves, inverse)
    return (
        pushed[0] - viscosity * square * state[0],
        pushed[1] - viscosity * square * state[1],
        pushed[2] - viscosity * square * state[2],
        -buoyancy_square * state[2] - diffusivity * square * state[3],
    )


def propagate(state, waves):
    square = squared(waves)
    inverse = 1.0 / jnp.maximum(square, 1.0)
    for half_step in range(2):
        anchor = state
        for order in (4.0, 3.0, 2.0, 1.0):
            rate = linear(state, waves, square, inverse)
            state = tuple(a + (0.5 * time_step / order) * r for a, r in zip(anchor, rate))
    return state


FIRST_ROW = 16
COARSE_ROWS = 8 * SCAN
TILE = 8 * 4
STEP = 4


def coarse_waves(plane, row0, rows):
    _, _, _, me = place()
    row = lax.broadcasted_iota(jnp.int32, (rows, N), 0) + row0
    lane = lax.broadcasted_iota(jnp.int32, (rows, N), 1) % 64
    wave_x = (me + GROUP * plane).astype(jnp.float32)
    wave_y = (row - KMAX).astype(jnp.float32)
    wave_z = (lane - KMAX).astype(jnp.float32)
    return wave_x, wave_y, wave_z


def coarse_inside(waves):
    wave_x, wave_y, wave_z = waves
    inside = (jnp.abs(wave_y) <= KCO) & (jnp.abs(wave_z) <= KCO)
    return inside & jnp.broadcast_to(wave_x <= KCO, inside.shape)


def packed(ref, plane, f):
    rows = pl.ds(f * KY + FIRST_ROW, COARSE_ROWS)
    lane = lax.broadcasted_iota(jnp.int32, (COARSE_ROWS, N), 1)
    real, imag = ref[plane, rows, :N], ref[plane, rows, N:]
    return jnp.where(lane < 64, real, pltpu.roll(imag, 64, 1))


class Passing:
    def __init__(self, refs):
        self.source, self.target, self.send, self.receive, self.own = refs

    def rows(self, owner, plane):
        slices = lax.axis_size("tm")
        return pl.ds(pl.multiple_of((plane * slices + owner) * TILE, TILE), TILE)

    def remote(self, i, plane, origin):
        tm, py, pz, _ = place()
        slices = lax.axis_size("tm")
        to = (tm + i) % slices
        where = (tm + slices - i) % slices if origin else tm
        return pltpu.make_async_remote_copy(
            src_ref=self.source.at[self.rows(to, plane), :],
            dst_ref=self.target.at[self.rows(where, plane), :],
            send_sem=self.send.at[plane * slices + i],
            recv_sem=self.receive.at[plane * slices + i],
            device_id=(to, py, pz),
            device_id_type=MESH,
        )

    def local(self, plane):
        tm, _, _, _ = place()
        part = self.rows(tm, plane)
        return pltpu.make_async_copy(
            self.source.at[part, :], self.target.at[part, :], self.own.at[plane]
        )


def whole_kernel(
    fields_hbm, fore_x_hbm, back_x_hbm, fore_y_hbm, back_y_hbm, fore_z_hbm, back_z_hbm,
    into4,
    fields, fore_x, back_x, fore_y, back_y, fore_z, back_z,
    load_sem, table_sem,
    out0, into0, send0, receive0, own0,
    out1, into1, send1, receive1, own1,
    out2, into2, send2, receive2, own2,
    out3, into3, send3, receive3, own3,
    out4, send4, receive4, own4,
    planes, first_modes, second_modes, start, fine, moved, matrix,
    coarse_out, coarse_in, coarse_send, coarse_receive, coarse_own,
    carry_out, carry_in, carry_send, carry_receive, carry_own,
):
    tm, py, pz, me = place()
    slices = lax.axis_size("tm")
    empty = jnp.zeros((2 * BLOCK, N), jnp.float32)
    into1[pl.ds(GRID_ROWS - 2 * BLOCK, 2 * BLOCK), :] = empty
    into4[pl.ds(GRID_ROWS - 2 * BLOCK, 2 * BLOCK), :] = empty
    coarse_in[...] = jnp.zeros_like(coarse_in)
    barrier = pltpu.get_barrier_semaphore()

    def greet(i, carry):
        peer = (tm, (py + i // 4) % 4, (pz + i % 4) % 4)
        pl.semaphore_signal(barrier, inc=1, device_id=peer, device_id_type=MESH)
        return carry

    lax.fori_loop(1, GROUP, greet, 0)

    def greet_slices(i, carry):
        peer = ((tm + i) % slices, py, pz)
        pl.semaphore_signal(barrier, inc=1, device_id=peer, device_id_type=MESH)
        return carry

    lax.fori_loop(1, slices, greet_slices, 0)

    loads = [
        pltpu.make_async_copy(held, ref, table_sem.at[i])
        for i, (held, ref) in enumerate(
            [
                (fore_x_hbm, fore_x),
                (fore_y_hbm, fore_y),
                (fore_z_hbm, fore_z),
                (back_z_hbm, back_z),
                (back_y_hbm, back_y),
                (back_x_hbm, back_x),
            ]
        )
    ]
    loads[0].start()

    def field_load(step):
        lines = pl.ds(pl.multiple_of(step * STEP, STEP), STEP)
        return pltpu.make_async_copy(
            fields_hbm.at[:, lines], fields.at[:, lines], load_sem.at[step]
        )

    def load(step, carry):
        field_load(step).start()
        return carry

    lax.fori_loop(0, BLOCK // STEP, load, 0)
    for copy in loads[1:]:
        copy.start()
    loads[0].wait()

    analysed = Exchange((out0, into0, send0, receive0, own0), True)
    to_grid = Exchange((out1, into1, send1, receive1, own1), False)
    to_modes = (
        Exchange((out2, into2, send2, receive2, own2), True),
        Exchange((out3, into3, send3, receive3, own3), True),
    )
    final = Exchange((out4, into4, send4, receive4, own4), False)
    coarse = Passing((coarse_out, coarse_in, coarse_send, coarse_receive, coarse_own))
    back = Passing((carry_out, carry_in, carry_send, carry_receive, carry_own))
    coarse_second = me + GROUP <= KCO

    def has_coarse(plane):
        return me + GROUP * plane <= KCO

    def analyse(step, carry):
        first = step * STEP
        field_load(step).wait()
        rows = [fields[f, first + y] for y in range(STEP) for f in range(4)]
        store_modes_x(jnp.concatenate(rows), fore_x, out0, first, STEP)
        return carry

    lax.fori_loop(0, BLOCK // STEP, analyse, 0)
    pl.semaphore_wait(barrier, GROUP - 1 + slices - 1)
    for plane in range(PLANES):
        analysed.start(plane)
    for copy in loads[1:]:
        copy.wait()

    def first_pass(plane, carry):
        analysed.arrived(plane)

        @pl.when(me + GROUP * plane <= KMAX)
        def _():
            first_modes[...] = fore_plane(into0, plane, planes, fore_y, fore_z)
            waves = waves_at(plane)
            inverse = 1.0 / jnp.maximum(squared(waves), 1.0)
            for part in range(2):
                lanes = slice(part * N, (part + 1) * N)
                state = [first_modes[f * KY : (f + 1) * KY, lanes] for f in range(4)]
                for f, value in enumerate(project(state[:3], waves, inverse) + (state[3],)):
                    start[plane, pl.ds(f * KY, KY), lanes] = value
            back_plane(start[plane], plane, out1, back_y, back_z)
            to_grid.start(plane)

        return carry

    lax.fori_loop(0, PLANES, first_pass, 0)

    def move(plane, carry):
        @pl.when(has_coarse(plane) & (tm > 0))
        def _():
            waves = coarse_waves(plane, FIRST_ROW, COARSE_ROWS)
            before = tuple(packed(start, plane, f) for f in range(4))
            for f, value in enumerate(propagate(before, waves)):
                moved[plane, f] = value

        @pl.when(has_coarse(plane) & (tm == 0))
        def _():
            moved[plane] = jnp.zeros((4, COARSE_ROWS, N), jnp.float32)

        waves = coarse_waves(plane, FIRST_ROW + tm * 8, 8)
        keep = coarse_inside(waves).astype(jnp.float32)
        zero = jnp.zeros((8, N), jnp.float32)
        for f in range(4):
            unit = tuple(zero + (1.0 if g == f else 0.0) for g in range(4))
            for g, value in enumerate(propagate(unit, waves)):
                matrix[plane, g * 4 + f] = keep * value
        return carry

    lax.fori_loop(0, 2, move, 0)

    def gather(plane, carry):
        to_grid.arrived(plane)
        return carry

    lax.fori_loop(0, PLANES, gather, 0)

    def lines(step, carry):
        first = step * STEP
        grid = load_fields_x(into1, back_x, first, STEP)
        one, two = [], []
        for y in range(STEP):
            u, v, w, b = (
                grid[y * N + f * BLOCK : y * N + (f + 1) * BLOCK] for f in range(4)
            )
            rest = w * w
            one += [u * u - rest, v * v - rest, u * v, u * w]
            two += [v * w, u * b, v * b, w * b]
        store_modes_x(jnp.concatenate(one), fore_x, out2, first, STEP)
        store_modes_x(jnp.concatenate(two), fore_x, out3, first, STEP)
        return carry

    lax.fori_loop(0, BLOCK // STEP, lines, 0)
    for plane in range(PLANES):
        for exchange in to_modes:
            exchange.start(plane)

    def second_pass(plane, carry):
        for exchange in to_modes:
            exchange.arrived(plane)

        @pl.when(me + GROUP * plane <= KMAX)
        def _():
            first_modes[...] = fore_plane(into2, plane, planes, fore_y, fore_z)
            second_modes[...] = fore_plane(into3, plane, planes, fore_y, fore_z)
            waves = waves_at(plane)
            wave_x, wave_y, wave_z = waves
            square = squared(waves)
            inverse = 1.0 / jnp.maximum(square, 1.0)
            for part in range(2):
                lanes = slice(part * N, (part + 1) * N)
                other = slice((1 - part) * N, (2 - part) * N)
                sign = 1.0 if part == 0 else -1.0
                xx, yy, xy, xz = (first_modes[f * KY : (f + 1) * KY, other] for f in range(4))
                yz, bx, by, bz = (second_modes[f * KY : (f + 1) * KY, other] for f in range(4))
                state = [start[plane, pl.ds(f * KY, KY), lanes] for f in range(4)]
                change = (
                    sign * (wave_x * xx + wave_y * xy + wave_z * xz),
                    sign * (wave_x * xy + wave_y * yy + wave_z * yz),
                    sign * (wave_x * xz + wave_y * yz),
                )
                lifted = sign * (wave_x * bx + wave_y * by + wave_z * bz)
                pushed = project(
                    (
                        change[0] + coriolis * state[1],
                        change[1] - coriolis * state[0],
                        change[2] + state[3],
                    ),
                    waves,
                    inverse,
                )
                rates = [pushed[f] - viscosity * square * state[f] for f in range(3)]
                rates.append(
                    lifted - buoyancy_square * state[2] - diffusivity * square * state[3]
                )
                for f in range(4):
                    fine[plane, pl.ds(f * KY, KY), lanes] = state[f] + time_step * rates[f]

        @pl.when(has_coarse(plane))
        def _():
            waves = coarse_waves(plane, FIRST_ROW, COARSE_ROWS)
            keep = coarse_inside(waves).astype(jnp.float32)
            for f in range(4):
                here = keep * packed(fine, plane, f) - keep * moved[plane, f]
                for tile in range(SCAN):
                    at = pl.multiple_of((plane * slices + tile) * TILE + f * 8, 8)
                    coarse_out[pl.ds(at, 8), :] = here[tile * 8 : tile * 8 + 8]

            def go(i, carry):
                @pl.when((tm + i) % slices < SCAN)
                def _():
                    coarse.remote(i, plane, False).start()

                return carry

            lax.fori_loop(1, slices, go, 0)

            @pl.when(tm < SCAN)
            def _():
                coarse.local(plane).start()

        @pl.when((plane == 1) & (tm < SCAN))
        def _():
            def wait(which):
                def go(i, carry):
                    coarse.remote(i, which, True).wait_recv()
                    return carry

                lax.fori_loop(1, slices, go, 0)
                coarse.local(which).wait()

            wait(0)

            @pl.when(coarse_second)
            def _():
                wait(1)

            def rows(n, which, f):
                return pl.ds(pl.multiple_of((which * slices + n) * TILE + f * 8, 8), 8)

            def step(n, state):
                new = []
                for which in range(2):
                    held = state[which * 4 : which * 4 + 4]
                    for g in range(4):
                        value = coarse_in[rows(n, which, g), :]
                        for f in range(4):
                            value = value + matrix[which, g * 4 + f] * held[f]
                        carry_out[rows(n, which, g), :] = value
                        new.append(value)
                return tuple(new)

            lax.fori_loop(0, slices, step, tuple([jnp.zeros((8, N), jnp.float32)] * 8))

            def send(which):
                def go(i, carry):
                    back.remote(i, which, False).start()
                    return carry

                lax.fori_loop(1, slices, go, 0)
                back.local(which).start()

            send(0)

            @pl.when(coarse_second)
            def _():
                send(1)

        return carry

    lax.fori_loop(0, PLANES, second_pass, 0)

    def last_pass(step, carry):
        plane = PLANES - 1 - step

        @pl.when(me + GROUP * plane <= KMAX)
        def _():
            @pl.when((plane < 2) & has_coarse(plane))
            def _():
                def wait(i, carry):
                    @pl.when((tm + slices - i) % slices < SCAN)
                    def _():
                        back.remote(i, plane, True).wait_recv()

                    return carry

                lax.fori_loop(1, slices, wait, 0)

                @pl.when(tm < SCAN)
                def _():
                    back.local(plane).wait()

                waves = coarse_waves(plane, FIRST_ROW, COARSE_ROWS)
                lane = lax.broadcasted_iota(jnp.int32, (COARSE_ROWS, N), 1)
                here = coarse_inside(waves) & (lane < 64)
                for f in range(4):
                    tiles = []
                    for tile in range(SCAN):
                        at = pl.multiple_of((plane * slices + tile) * TILE + f * 8, 8)
                        tiles.append(carry_in[pl.ds(at, 8), :])
                    value = jnp.concatenate(tiles)
                    rows = pl.ds(f * KY + FIRST_ROW, COARSE_ROWS)
                    fine[plane, rows, :N] = jnp.where(here, value, fine[plane, rows, :N])
                    fine[plane, rows, N:] = jnp.where(
                        here, pltpu.roll(value, 64, 1), fine[plane, rows, N:]
                    )

            back_plane(fine[plane], plane, out4, back_y, back_z)
            final.start(plane)

        return carry

    lax.fori_loop(0, PLANES, last_pass, 0)

    def done(plane, carry):
        analysed.sent(plane)
        to_grid.sent(plane)
        for exchange in to_modes:
            exchange.sent(plane)
        final.sent(plane)
        final.arrived(plane)
        return carry

    lax.fori_loop(0, PLANES, done, 0)

    def passed(q, carry):
        plane, i = q // slices, q % slices

        @pl.when((i > 0) & has_coarse(plane))
        def _():
            @pl.when((tm + i) % slices < SCAN)
            def _():
                coarse.remote(i, plane, False).wait_send()

            @pl.when(tm < SCAN)
            def _():
                back.remote(i, plane, False).wait_send()

        return carry

    lax.fori_loop(0, 2 * slices, passed, 0)


def lines_kernel(modes, back_x, out):
    grid = load_fields_x(modes, back_x, pl.program_id(0) * STEP, STEP)
    for y in range(STEP):
        for f in range(4):
            at = y * N + f * BLOCK
            out[f, y] = grid[at : at + BLOCK]


def on_device(state_old):
    slices = lax.axis_size("tm")
    fields = state_old[0]
    held = [jnp.asarray(table) for table in tables()]
    inputs = [pltpu.with_memory_space_constraint(a, pltpu.HBM) for a in [fields] + held]
    half = pltpu.VMEM((4 * KY, 2 * N), jnp.float32)
    modes = pltpu.VMEM((PLANES, 4 * KY, 2 * N), jnp.float32)
    passing = [
        pltpu.VMEM((2 * slices * TILE, N), jnp.float32),
        pltpu.VMEM((2 * slices * TILE, N), jnp.float32),
        pltpu.SemaphoreType.DMA((2 * slices,)),
        pltpu.SemaphoreType.DMA((2 * slices,)),
        pltpu.SemaphoreType.DMA((2,)),
    ]
    last = exchange_scratch(False)
    arrived = pl.pallas_call(
        whole_kernel,
        name="whole",
        out_shape=jax.ShapeDtypeStruct((GRID_ROWS, N), jnp.float32),
        in_specs=[pl.BlockSpec(memory_space=pltpu.HBM)] * len(inputs),
        out_specs=pl.BlockSpec(memory_space=pltpu.VMEM),
        scratch_shapes=[pltpu.VMEM(a.shape, a.dtype) for a in inputs]
        + [
            pltpu.SemaphoreType.DMA((BLOCK // STEP,)),
            pltpu.SemaphoreType.DMA((len(held),)),
        ]
        + exchange_scratch(True)
        + exchange_scratch(False)
        + exchange_scratch(True)
        + exchange_scratch(True)
        + [last[0]]
        + last[2:]
        + [
            pltpu.VMEM((2, 2 * N, 2 * N), jnp.float32),
            half,
            half,
            modes,
            modes,
            pltpu.VMEM((2, 4, COARSE_ROWS, N), jnp.float32),
            pltpu.VMEM((2, 16, 8, N), jnp.float32),
        ]
        + passing
        + passing,
        compiler_params=pltpu.CompilerParams(
            collective_id=0, has_side_effects=True, vmem_limit_bytes=VMEM_BYTES
        ),
    )(*inputs)
    result = pl.pallas_call(
        lines_kernel,
        name="lines",
        grid=(BLOCK // STEP,),
        out_shape=jax.ShapeDtypeStruct(fields.shape, jnp.float32),
        in_specs=[pl.BlockSpec(memory_space=pltpu.VMEM)] * 2,
        out_specs=pl.BlockSpec((4, STEP, BLOCK, N), lambda i: (0, i, 0, 0)),
        compiler_params=pltpu.CompilerParams(vmem_limit_bytes=16 << 20),
    )(arrived, held[1])
    return result[None]


def solution(mesh):
    return jax.shard_map(
        on_device,
        mesh=mesh,
        in_specs=(P("tm", None, "py", "pz", None),),
        out_specs=P("tm", None, "py", "pz", None),
        check_vma=False,
    )
```

```python
import functools

import jax
import jax.numpy as jnp
import numpy as np
from jax import lax
from jax.experimental import pallas as pl
from jax.experimental.pallas import tpu as pltpu
from jax.sharding import PartitionSpec as P

KMAX = 42
KCO = 21
N = 128
KY = 96
PLANES = 3
GROUP = 16
BLOCK = 32
MODE_ROWS = 88
HOLDERS = KMAX + 1 - 2 * GROUP
KZ = 2 * KMAX + 1
EMPTY = PLANES * GROUP - KMAX - 1
THIN = N // GROUP
SYNTH_PACKS = 6
PRODUCT_PACKS = 11
SPECTRAL_ROWS = 2 * PLANES * GROUP * BLOCK
GRID_ROWS = MODE_ROWS * BLOCK
PLANE_ROWS = PLANES * GROUP * 2 * BLOCK
SCAN = 6
ORDER = (
    (2, 2), (2, 3), (1, 2), (3, 2), (1, 3), (3, 3), (2, 0), (2, 1),
    (0, 2), (0, 3), (1, 0), (3, 0), (1, 1), (3, 1), (0, 1),
)
MESH = pl.DeviceIdType.MESH
VMEM_BYTES = 50 << 20

time_step = 0.01
coriolis = 6.0
buoyancy_square = 100.0
viscosity = 0.001
diffusivity = 0.001


def halves(table):
    exact = np.asarray(table, np.float32)
    high = exact.astype(jnp.bfloat16)
    low = (exact - high.astype(np.float32)).astype(jnp.bfloat16)
    return high, low


def tables():
    scale = N**-0.5
    cells = np.arange(N)
    waves_x = np.arange(PLANES * GROUP)
    angle = 2 * np.pi / N * ((waves_x[:, None] * cells) % N)
    inside = (waves_x <= KMAX)[:, None] * scale
    fore = np.stack([np.cos(angle), -np.sin(angle)], axis=1) * inside[:, None]
    weight = np.where(waves_x == 0, 1.0, 2.0)[:, None, None]
    back = fore * weight
    rest = ((0, N - 2 * PLANES * GROUP), (0, 0))
    fore = np.pad(fore.reshape(-1, N), rest).T
    back = np.pad(back.reshape(-1, N), rest)

    def one_pass(table):
        high, low = halves(table)
        return np.concatenate(
            [
                np.concatenate([high, low], axis=1),
                np.concatenate([high, np.zeros_like(high)], axis=1),
            ]
        )

    def pair(slots):
        waves = np.arange(slots) - KMAX
        angle = 2 * np.pi / N * ((waves[:, None] * cells[None, :]) % N)
        inside = (waves <= KMAX)[:, None] * scale
        return np.cos(angle) * inside, np.sin(angle) * inside

    cos_y, sin_y = pair(KY)
    cos_z, sin_z = pair(N)
    fore_y = np.block([[cos_y, sin_y], [-sin_y, cos_y]])
    back_y = np.block([[cos_y.T, -sin_y.T], [sin_y.T, cos_y.T]])
    fore_z = np.block([[cos_z.T, -sin_z.T], [sin_z.T, cos_z.T]])
    back_z = np.block([[cos_z, sin_z], [-sin_z, cos_z]])
    stack = lambda table: np.concatenate(halves(table))
    return (
        one_pass(fore),
        one_pass(back),
        stack(fore_y),
        stack(back_y),
        stack(fore_z),
        stack(back_z),
    )


def split(values):
    high = values.astype(jnp.bfloat16)
    low = (values - high.astype(jnp.float32)).astype(jnp.bfloat16)
    return high, low


def mul(left, right):
    return jnp.dot(left, right, preferred_element_type=jnp.float32)


def by_x(values, table):
    out = mul(jnp.concatenate(split(values), axis=1), table[...])
    return out[:, :N] + out[:, N:]


def by_left(table, values):
    rows = table.shape[0] // 2
    high, low = split(values)
    out = mul(table[...], high)
    return out[:rows] + out[rows:] + mul(table[:rows], low)


def by_right(values, table):
    rows = table.shape[0] // 2
    high, low = split(values)
    return mul(high, table[:rows]) + mul(low, table[:rows]) + mul(high, table[rows:])


def swap_groups(parts):
    lane = lax.broadcasted_iota(jnp.int32, parts[0].shape, 1)
    low_half = lane < 64
    even = (lane // 32) % 2 == 0
    a0, a1, a2, a3 = parts
    p0 = jnp.where(low_half, a0, pltpu.roll(a2, 64, 1))
    p2 = jnp.where(low_half, pltpu.roll(a0, 64, 1), a2)
    p1 = jnp.where(low_half, a1, pltpu.roll(a3, 64, 1))
    p3 = jnp.where(low_half, pltpu.roll(a1, 64, 1), a3)
    return (
        jnp.where(even, p0, pltpu.roll(p1, 32, 1)),
        jnp.where(even, pltpu.roll(p0, 96, 1), p1),
        jnp.where(even, p2, pltpu.roll(p3, 32, 1)),
        jnp.where(even, pltpu.roll(p2, 96, 1), p3),
    )


def place():
    tm, py, pz = lax.axis_index("tm"), lax.axis_index("py"), lax.axis_index("pz")
    return tm, py, pz, py * 4 + pz


def rows_at(start, count):
    return pl.ds(pl.multiple_of(start, 8), count)


class Exchange:
    def __init__(self, refs, to_modes, rows):
        self.source, self.target, self.send, self.receive, self.own = refs
        self.to_modes, self.rows = to_modes, rows

    def chunk(self, owner, plane):
        return rows_at((plane * GROUP + owner) * self.rows, self.rows)

    def local(self, plane):
        _, _, _, me = place()
        part = self.chunk(me, plane)
        return pltpu.make_async_copy(
            self.source.at[part, :], self.target.at[part, :], self.own.at[plane]
        )

    def remote(self, step, plane):
        tm, py, pz, me = place()
        to_y, to_z = (py + step[0]) % 4, (pz + step[1]) % 4
        return pltpu.make_async_remote_copy(
            src_ref=self.source.at[self.chunk(to_y * 4 + to_z, plane), :],
            dst_ref=self.target.at[self.chunk(me, plane), :],
            send_sem=self.send.at[plane],
            recv_sem=self.receive.at[plane],
            device_id=(tm, to_y, to_z),
            device_id_type=MESH,
        )

    def amount(self, count, plane):
        tm, py, pz, _ = place()
        rows = pl.ds(0, count * self.rows)
        return pltpu.make_async_remote_copy(
            src_ref=self.source.at[rows, :],
            dst_ref=self.target.at[rows, :],
            send_sem=self.send.at[plane],
            recv_sem=self.receive.at[plane],
            device_id=(tm, (py + 1) % 4, pz),
            device_id_type=MESH,
        )

    def start(self, plane):
        _, py, pz, me = place()

        def go(step):
            to = (py + step[0]) % 4 * 4 + (pz + step[1]) % 4
            if not self.to_modes or (isinstance(plane, int) and plane < PLANES - 1):
                self.remote(step, plane).start()
            else:
                pl.when(to + GROUP * plane <= KMAX)(lambda: self.remote(step, plane).start())

        def all_steps():
            for step in ORDER:
                go(step)

        if self.to_modes:
            all_steps()

        @pl.when(me + GROUP * plane <= KMAX)
        def _():
            if not self.to_modes:
                all_steps()
            self.local(plane).start()

    def modes_side(self, plane, done):
        _, _, _, me = place()

        @pl.when(me + GROUP * plane <= KMAX)
        def _():
            done(self.amount(GROUP - 1, plane))

    def grid_side(self, plane, done):
        _, _, _, me = place()

        @pl.when(plane < PLANES - 1)
        def _():
            done(self.amount(GROUP - 1, plane))

        @pl.when((plane == PLANES - 1) & (me < HOLDERS))
        def _():
            done(self.amount(HOLDERS - 1, plane))

        @pl.when((plane == PLANES - 1) & (me >= HOLDERS))
        def _():
            done(self.amount(HOLDERS, plane))

    def arrived(self, plane):
        _, _, _, me = place()
        side = self.modes_side if self.to_modes else self.grid_side
        side(plane, lambda copy: copy.wait_recv())

        @pl.when(me + GROUP * plane <= KMAX)
        def _():
            self.local(plane).wait()

    def sent(self, plane):
        side = self.grid_side if self.to_modes else self.modes_side
        side(plane, lambda copy: copy.wait_send())


def exchange_scratch(source, target):
    return [
        pltpu.VMEM((source, N), jnp.float32),
        pltpu.VMEM((target, N), jnp.float32),
        pltpu.SemaphoreType.DMA((PLANES,)),
        pltpu.SemaphoreType.DMA((PLANES,)),
        pltpu.SemaphoreType.DMA((PLANES,)),
    ]


def store_modes_x(fields, table, target, first, count, gap=1):
    modes = by_x(fields, table)
    for y in range(count):
        turned = modes[y * N : (y + 1) * N].T
        target[pl.ds(first + y * gap, MODE_ROWS, stride=BLOCK), :] = turned[:MODE_ROWS]


def load_fields_x(source, table, first, count, gap=1):
    lines = []
    for y in range(count):
        rows = source[pl.ds(first + y * gap, MODE_ROWS, stride=BLOCK), :]
        rows = jnp.concatenate([rows, jnp.zeros((N - MODE_ROWS, N), jnp.float32)])
        lines.append(rows.T)
    return by_x(jnp.concatenate(lines), table)


def fore_plane(received, plane, planes, fore_y, fore_z):
    for part in range(2):
        for block in range(4):
            blocks = []
            for s in range(4):
                start = ((plane * GROUP + block * 4 + s) * 2 + part) * BLOCK
                blocks.append(received[pl.ds(pl.multiple_of(start, BLOCK), BLOCK), :])
            for f, piece in enumerate(swap_groups(blocks)):
                rows = pl.ds(part * N + block * BLOCK, BLOCK)
                planes[f // 2, rows, (f % 2) * N : (f % 2 + 1) * N] = piece
    lines = []
    for duo in range(2):
        along_y = by_left(fore_y, planes[duo])
        for f in range(2):
            own = along_y[:, f * N : (f + 1) * N]
            lines.append(jnp.concatenate([own[:KY], own[KY:]], axis=1))
    return by_right(jnp.concatenate(lines), fore_z)


def back_plane(modes, plane, target, back_y, back_z):
    along_z = by_right(modes, back_z)
    fields = []
    for duo in range(2):
        both = []
        for f in range(2):
            own = along_z[(2 * duo + f) * KY : (2 * duo + f + 1) * KY]
            both.append(jnp.concatenate([own[:, :N], own[:, N:]]))
        along_y = by_left(back_y, jnp.concatenate(both, axis=1))
        fields += [along_y[:, :N], along_y[:, N:]]
    for part in range(2):
        for block in range(4):
            rows = slice(part * N + block * BLOCK, part * N + (block + 1) * BLOCK)
            for s, piece in enumerate(swap_groups([field[rows] for field in fields])):
                start = ((plane * GROUP + block * 4 + s) * 2 + part) * BLOCK
                target[pl.ds(pl.multiple_of(start, BLOCK), BLOCK), :] = piece


def pack(pieces):
    out = []
    whole = len(pieces) // 3 * 3
    for first in range(0, whole, 3):
        one, two, three = pieces[first : first + 3]
        lane = lax.broadcasted_iota(jnp.int32, one.shape, 1)
        turned = pltpu.roll(two, KZ, 1)
        out.append(jnp.where(lane < KZ, one, turned))
        out.append(jnp.where(lane < 2 * KZ - N, turned, pltpu.roll(three, 2 * KZ - N, 1)))
    return out + list(pieces[whole:])


def unpack(packs, count):
    out = []
    for first in range(0, count // 3 * 2, 2):
        one, two = packs[first : first + 2]
        lane = lax.broadcasted_iota(jnp.int32, one.shape, 1)
        out.append(one)
        out.append(pltpu.roll(jnp.where(lane < 2 * KZ - N, two, one), N - KZ, 1))
        out.append(pltpu.roll(two, 2 * N - 2 * KZ, 1))
    return out + list(packs[count // 3 * 2 :])


def beside(left, right):
    return jnp.concatenate([left, right], axis=1)


def spread_packs(packs, plane, target):
    for owner in range(GROUP):
        for k, values in enumerate(packs):
            start = ((plane * GROUP + owner) * len(packs) + k) * THIN
            target[rows_at(start, THIN), :] = values[owner * THIN : (owner + 1) * THIN]


def gather_packs(source, plane, count):
    packs = []
    for k in range(count):
        starts = [((plane * GROUP + owner) * count + k) * THIN for owner in range(GROUP)]
        packs.append(jnp.concatenate([source[rows_at(at, THIN), :] for at in starts]))
    return packs


def back_along_y(values, plane, target, back_y):
    pieces = []
    for duo in range(2):
        both = []
        for f in (2 * duo, 2 * duo + 1):
            own = values[f * KY : (f + 1) * KY]
            both.append(jnp.concatenate([own[:, :N], own[:, N:]]))
        along = by_left(back_y, beside(*both))
        pieces += [along[:N, :N], along[N:, :N], along[:N, N:], along[N:, N:]]
    spread_packs(pack(pieces), plane, target)


def back_along_z(source, plane, spectral, back_z):
    pieces = unpack(gather_packs(source, plane, SYNTH_PACKS), 8)
    lines = [beside(pieces[2 * f], pieces[2 * f + 1]) for f in range(4)]
    along = by_right(jnp.concatenate(lines), back_z)
    for owner in range(GROUP):
        for f in range(4):
            rows = slice(f * N + owner * THIN, f * N + (owner + 1) * THIN)
            for c in range(2):
                start = ((plane * GROUP + owner) * 2 + c) * BLOCK + f * THIN
                spectral[rows_at(start, THIN), :] = along[rows, c * N : (c + 1) * N]


def fore_along_z(spectral, plane, target, fore_z):
    pieces = []
    for ref in spectral:
        lines = []
        for owner in range(GROUP):
            start = (plane * GROUP + owner) * 2 * BLOCK
            both = [ref[rows_at(start + c * BLOCK, BLOCK), :] for c in range(2)]
            lines.append(beside(*both))
        along = by_right(jnp.concatenate(lines), fore_z)
        for f in range(4):
            for c in range(2):
                pieces.append(
                    jnp.concatenate(
                        [
                            along[
                                owner * BLOCK + f * THIN : owner * BLOCK + (f + 1) * THIN,
                                c * N : (c + 1) * N,
                            ]
                            for owner in range(GROUP)
                        ]
                    )
                )
    spread_packs(pack(pieces), plane, target)


def fore_along_y(source, plane, modes, fore_y):
    pieces = unpack(gather_packs(source, plane, PRODUCT_PACKS), 16)
    for duo in range(4):
        both = [
            jnp.concatenate([pieces[2 * f], pieces[2 * f + 1]])
            for f in (2 * duo, 2 * duo + 1)
        ]
        along = by_left(fore_y, beside(*both))
        ref = modes[duo // 2]
        for half in range(2):
            rows = slice((duo % 2 * 2 + half) * KY, (duo % 2 * 2 + half + 1) * KY)
            own = along[:, half * N : (half + 1) * N]
            ref[rows, :N] = own[:KY]
            ref[rows, N:] = own[KY:]


def waves_at(plane):
    _, _, _, me = place()
    wave_x = (me + GROUP * plane).astype(jnp.float32)
    wave_y = (lax.broadcasted_iota(jnp.int32, (KY, N), 0) - KMAX).astype(jnp.float32)
    wave_z = (lax.broadcasted_iota(jnp.int32, (KY, N), 1) - KMAX).astype(jnp.float32)
    return wave_x, wave_y, wave_z


def squared(waves):
    wave_x, wave_y, wave_z = waves
    return wave_x * wave_x + wave_y * wave_y + wave_z * wave_z


def project(velocity, waves, inverse):
    wave_x, wave_y, wave_z = waves
    along = (wave_x * velocity[0] + wave_y * velocity[1] + wave_z * velocity[2]) * inverse
    return (
        velocity[0] - wave_x * along,
        velocity[1] - wave_y * along,
        velocity[2] - wave_z * along,
    )


def linear(state, waves, square, inverse):
    pushed = project((coriolis * state[1], -coriolis * state[0], state[3]), waves, inverse)
    return (
        pushed[0] - viscosity * square * state[0],
        pushed[1] - viscosity * square * state[1],
        pushed[2] - viscosity * square * state[2],
        -buoyancy_square * state[2] - diffusivity * square * state[3],
    )


def propagate(state, waves):
    square = squared(waves)
    inverse = 1.0 / jnp.maximum(square, 1.0)
    for half_step in range(2):
        anchor = state
        for order in (4.0, 3.0, 2.0, 1.0):
            rate = linear(state, waves, square, inverse)
            state = tuple(a + (0.5 * time_step / order) * r for a, r in zip(anchor, rate))
    return state


FIRST_ROW = 16
COARSE_ROWS = 8 * SCAN
TILE = 8 * 4
STEP = 4


def coarse_waves(plane, row0, rows):
    _, _, _, me = place()
    row = lax.broadcasted_iota(jnp.int32, (rows, N), 0) + row0
    lane = lax.broadcasted_iota(jnp.int32, (rows, N), 1) % 64
    wave_x = (me + GROUP * plane).astype(jnp.float32)
    wave_y = (row - KMAX).astype(jnp.float32)
    wave_z = (lane - KMAX).astype(jnp.float32)
    return wave_x, wave_y, wave_z


def coarse_inside(waves):
    wave_x, wave_y, wave_z = waves
    inside = (jnp.abs(wave_y) <= KCO) & (jnp.abs(wave_z) <= KCO)
    return inside & jnp.broadcast_to(wave_x <= KCO, inside.shape)


def packed(ref, plane, f):
    rows = pl.ds(f * KY + FIRST_ROW, COARSE_ROWS)
    lane = lax.broadcasted_iota(jnp.int32, (COARSE_ROWS, N), 1)
    real, imag = ref[plane, rows, :N], ref[plane, rows, N:]
    return jnp.where(lane < 64, real, pltpu.roll(imag, 64, 1))


class Passing:
    def __init__(self, refs):
        self.source, self.target, self.send, self.receive, self.own = refs

    def rows(self, owner, plane):
        slices = lax.axis_size("tm")
        return pl.ds(pl.multiple_of((plane * slices + owner) * TILE, TILE), TILE)

    def remote(self, i, plane, origin):
        tm, py, pz, _ = place()
        slices = lax.axis_size("tm")
        to = (tm + i) % slices
        where = (tm + slices - i) % slices if origin else tm
        return pltpu.make_async_remote_copy(
            src_ref=self.source.at[self.rows(to, plane), :],
            dst_ref=self.target.at[self.rows(where, plane), :],
            send_sem=self.send.at[plane * slices + i],
            recv_sem=self.receive.at[plane * slices + i],
            device_id=(to, py, pz),
            device_id_type=MESH,
        )

    def local(self, plane):
        tm, _, _, _ = place()
        part = self.rows(tm, plane)
        return pltpu.make_async_copy(
            self.source.at[part, :], self.target.at[part, :], self.own.at[plane]
        )


def whole_kernel(
    fields_hbm, fore_x_hbm, back_x_hbm, fore_y_hbm, back_y_hbm, fore_z_hbm, back_z_hbm,
    into4,
    fields, fore_x, back_x, fore_y, back_y, fore_z, back_z,
    load_sem, table_sem,
    out0, into0, send0, receive0, own0,
    out1, into1, send1, receive1, own1,
    out2, into2, send2, receive2, own2,
    out4, send4, receive4, own4,
    synth, first_products, second_products,
    planes, first_modes, second_modes, start, fine, moved, matrix,
    coarse_out, coarse_in, coarse_send, coarse_receive, coarse_own,
    carry_out, carry_in, carry_send, carry_receive, carry_own,
):
    tm, py, pz, me = place()
    slices = lax.axis_size("tm")
    empty = jnp.zeros((2 * BLOCK, N), jnp.float32)
    into1[pl.ds((KMAX + 1) * SYNTH_PACKS * THIN, EMPTY * SYNTH_PACKS * THIN), :] = jnp.zeros(
        (EMPTY * SYNTH_PACKS * THIN, N), jnp.float32
    )
    into4[pl.ds(GRID_ROWS - 2 * BLOCK, 2 * BLOCK), :] = empty
    coarse_in[...] = jnp.zeros_like(coarse_in)
    barrier = pltpu.get_barrier_semaphore()

    def greet(i, carry):
        peer = (tm, (py + i // 4) % 4, (pz + i % 4) % 4)
        pl.semaphore_signal(barrier, inc=1, device_id=peer, device_id_type=MESH)
        return carry

    lax.fori_loop(1, GROUP, greet, 0)

    def greet_slices(i, carry):
        peer = ((tm + i) % slices, py, pz)
        pl.semaphore_signal(barrier, inc=1, device_id=peer, device_id_type=MESH)
        return carry

    lax.fori_loop(1, slices, greet_slices, 0)

    loads = [
        pltpu.make_async_copy(held, ref, table_sem.at[i])
        for i, (held, ref) in enumerate(
            [
                (fore_x_hbm, fore_x),
                (fore_y_hbm, fore_y),
                (fore_z_hbm, fore_z),
                (back_z_hbm, back_z),
                (back_y_hbm, back_y),
                (back_x_hbm, back_x),
            ]
        )
    ]
    loads[0].start()

    def field_load(step):
        lines = pl.ds(pl.multiple_of(step * STEP, STEP), STEP)
        return pltpu.make_async_copy(
            fields_hbm.at[:, lines], fields.at[:, lines], load_sem.at[step]
        )

    def load(step, carry):
        field_load(step).start()
        return carry

    lax.fori_loop(0, BLOCK // STEP, load, 0)
    for copy in loads[1:]:
        copy.start()
    loads[0].wait()

    analysed = Exchange((out0, into0, send0, receive0, own0), True, 2 * BLOCK)
    to_grid = Exchange((out1, into1, send1, receive1, own1), False, SYNTH_PACKS * THIN)
    to_modes = Exchange((out2, into2, send2, receive2, own2), True, PRODUCT_PACKS * THIN)
    final = Exchange((out4, into4, send4, receive4, own4), False, 2 * BLOCK)
    coarse = Passing((coarse_out, coarse_in, coarse_send, coarse_receive, coarse_own))
    back = Passing((carry_out, carry_in, carry_send, carry_receive, carry_own))
    coarse_second = me + GROUP <= KCO

    def has_coarse(plane):
        return me + GROUP * plane <= KCO

    def analyse(step, carry):
        first = step * STEP
        field_load(step).wait()
        rows = [fields[f, first + y] for y in range(STEP) for f in range(4)]
        store_modes_x(jnp.concatenate(rows), fore_x, out0, first, STEP)
        return carry

    lax.fori_loop(0, BLOCK // STEP, analyse, 0)
    pl.semaphore_wait(barrier, GROUP - 1 + slices - 1)
    for plane in range(PLANES):
        analysed.start(plane)
    for copy in loads[1:]:
        copy.wait()

    def first_pass(plane, carry):
        analysed.arrived(plane)

        @pl.when(me + GROUP * plane <= KMAX)
        def _():
            first_modes[...] = fore_plane(into0, plane, planes, fore_y, fore_z)
            waves = waves_at(plane)
            inverse = 1.0 / jnp.maximum(squared(waves), 1.0)
            for part in range(2):
                lanes = slice(part * N, (part + 1) * N)
                state = [first_modes[f * KY : (f + 1) * KY, lanes] for f in range(4)]
                for f, value in enumerate(project(state[:3], waves, inverse) + (state[3],)):
                    start[plane, pl.ds(f * KY, KY), lanes] = value
            back_along_y(start[plane], plane, out1, back_y)
            to_grid.start(plane)

        return carry

    lax.fori_loop(0, PLANES, first_pass, 0)

    def move(plane, carry):
        @pl.when(has_coarse(plane) & (tm > 0))
        def _():
            waves = coarse_waves(plane, FIRST_ROW, COARSE_ROWS)
            before = tuple(packed(start, plane, f) for f in range(4))
            for f, value in enumerate(propagate(before, waves)):
                moved[plane, f] = value

        @pl.when(has_coarse(plane) & (tm == 0))
        def _():
            moved[plane] = jnp.zeros((4, COARSE_ROWS, N), jnp.float32)

        waves = coarse_waves(plane, FIRST_ROW + tm * 8, 8)
        keep = coarse_inside(waves).astype(jnp.float32)
        zero = jnp.zeros((8, N), jnp.float32)
        for f in range(4):
            unit = tuple(zero + (1.0 if g == f else 0.0) for g in range(4))
            for g, value in enumerate(propagate(unit, waves)):
                matrix[plane, g * 4 + f] = keep * value
        return carry

    lax.fori_loop(0, 2, move, 0)

    def gather(plane, carry):
        to_grid.arrived(plane)
        back_along_z(into1, plane, synth, back_z)
        return carry

    lax.fori_loop(0, PLANES, gather, 0)

    def lines(y, carry):
        grid = load_fields_x(synth, back_x, y, 4, THIN)
        u, v, w, b = (grid[f * N : (f + 1) * N] for f in range(4))
        rest = w * w
        one = [u * u - rest, v * v - rest, u * v, u * w]
        two = [v * w, u * b, v * b, w * b]
        store_modes_x(jnp.concatenate(one), fore_x, first_products, y, 4, THIN)
        store_modes_x(jnp.concatenate(two), fore_x, second_products, y, 4, THIN)
        return carry

    lax.fori_loop(0, THIN, lines, 0)

    def scatter(plane, carry):
        fore_along_z((first_products, second_products), plane, out2, fore_z)
        to_modes.start(plane)
        return carry

    lax.fori_loop(0, PLANES, scatter, 0)

    def second_pass(plane, carry):
        to_modes.arrived(plane)

        @pl.when(me + GROUP * plane <= KMAX)
        def _():
            fore_along_y(into2, plane, (first_modes, second_modes), fore_y)
            waves = waves_at(plane)
            wave_x, wave_y, wave_z = waves
            square = squared(waves)
            inverse = 1.0 / jnp.maximum(square, 1.0)
            for part in range(2):
                lanes = slice(part * N, (part + 1) * N)
                other = slice((1 - part) * N, (2 - part) * N)
                sign = 1.0 if part == 0 else -1.0
                xx, yy, xy, xz = (first_modes[f * KY : (f + 1) * KY, other] for f in range(4))
                yz, bx, by, bz = (second_modes[f * KY : (f + 1) * KY, other] for f in range(4))
                state = [start[plane, pl.ds(f * KY, KY), lanes] for f in range(4)]
                change = (
                    sign * (wave_x * xx + wave_y * xy + wave_z * xz),
                    sign * (wave_x * xy + wave_y * yy + wave_z * yz),
                    sign * (wave_x * xz + wave_y * yz),
                )
                lifted = sign * (wave_x * bx + wave_y * by + wave_z * bz)
                pushed = project(
                    (
                        change[0] + coriolis * state[1],
                        change[1] - coriolis * state[0],
                        change[2] + state[3],
                    ),
                    waves,
                    inverse,
                )
                rates = [pushed[f] - viscosity * square * state[f] for f in range(3)]
                rates.append(
                    lifted - buoyancy_square * state[2] - diffusivity * square * state[3]
                )
                for f in range(4):
                    fine[plane, pl.ds(f * KY, KY), lanes] = state[f] + time_step * rates[f]

        @pl.when(has_coarse(plane))
        def _():
            waves = coarse_waves(plane, FIRST_ROW, COARSE_ROWS)
            keep = coarse_inside(waves).astype(jnp.float32)
            for f in range(4):
                here = keep * packed(fine, plane, f) - keep * moved[plane, f]
                for tile in range(SCAN):
                    at = pl.multiple_of((plane * slices + tile) * TILE + f * 8, 8)
                    coarse_out[pl.ds(at, 8), :] = here[tile * 8 : tile * 8 + 8]

            def go(i, carry):
                @pl.when((tm + i) % slices < SCAN)
                def _():
                    coarse.remote(i, plane, False).start()

                return carry

            lax.fori_loop(1, slices, go, 0)

            @pl.when(tm < SCAN)
            def _():
                coarse.local(plane).start()

        @pl.when((plane == 1) & (tm < SCAN))
        def _():
            def wait(which):
                def go(i, carry):
                    coarse.remote(i, which, True).wait_recv()
                    return carry

                lax.fori_loop(1, slices, go, 0)
                coarse.local(which).wait()

            wait(0)

            @pl.when(coarse_second)
            def _():
                wait(1)

            def rows(n, which, f):
                return pl.ds(pl.multiple_of((which * slices + n) * TILE + f * 8, 8), 8)

            def step(n, state):
                new = []
                for which in range(2):
                    held = state[which * 4 : which * 4 + 4]
                    for g in range(4):
                        value = coarse_in[rows(n, which, g), :]
                        for f in range(4):
                            value = value + matrix[which, g * 4 + f] * held[f]
                        carry_out[rows(n, which, g), :] = value
                        new.append(value)
                return tuple(new)

            lax.fori_loop(0, slices, step, tuple([jnp.zeros((8, N), jnp.float32)] * 8))

            def send(which):
                def go(i, carry):
                    back.remote(i, which, False).start()
                    return carry

                lax.fori_loop(1, slices, go, 0)
                back.local(which).start()

            send(0)

            @pl.when(coarse_second)
            def _():
                send(1)

        return carry

    lax.fori_loop(0, PLANES, second_pass, 0)

    def last_pass(step, carry):
        plane = PLANES - 1 - step

        @pl.when(me + GROUP * plane <= KMAX)
        def _():
            @pl.when((plane < 2) & has_coarse(plane))
            def _():
                def wait(i, carry):
                    @pl.when((tm + slices - i) % slices < SCAN)
                    def _():
                        back.remote(i, plane, True).wait_recv()

                    return carry

                lax.fori_loop(1, slices, wait, 0)

                @pl.when(tm < SCAN)
                def _():
                    back.local(plane).wait()

                waves = coarse_waves(plane, FIRST_ROW, COARSE_ROWS)
                lane = lax.broadcasted_iota(jnp.int32, (COARSE_ROWS, N), 1)
                here = coarse_inside(waves) & (lane < 64)
                for f in range(4):
                    tiles = []
                    for tile in range(SCAN):
                        at = pl.multiple_of((plane * slices + tile) * TILE + f * 8, 8)
                        tiles.append(carry_in[pl.ds(at, 8), :])
                    value = jnp.concatenate(tiles)
                    rows = pl.ds(f * KY + FIRST_ROW, COARSE_ROWS)
                    fine[plane, rows, :N] = jnp.where(here, value, fine[plane, rows, :N])
                    fine[plane, rows, N:] = jnp.where(
                        here, pltpu.roll(value, 64, 1), fine[plane, rows, N:]
                    )

            back_plane(fine[plane], plane, out4, back_y, back_z)
            final.start(plane)

        return carry

    lax.fori_loop(0, PLANES, last_pass, 0)

    def done(plane, carry):
        analysed.sent(plane)
        to_grid.sent(plane)
        to_modes.sent(plane)
        final.sent(plane)
        final.arrived(plane)
        return carry

    lax.fori_loop(0, PLANES, done, 0)

    def passed(q, carry):
        plane, i = q // slices, q % slices

        @pl.when((i > 0) & has_coarse(plane))
        def _():
            @pl.when((tm + i) % slices < SCAN)
            def _():
                coarse.remote(i, plane, False).wait_send()

            @pl.when(tm < SCAN)
            def _():
                back.remote(i, plane, False).wait_send()

        return carry

    lax.fori_loop(0, 2 * slices, passed, 0)


def lines_kernel(modes, back_x, out):
    grid = load_fields_x(modes, back_x, pl.program_id(0) * STEP, STEP)
    for y in range(STEP):
        for f in range(4):
            at = y * N + f * BLOCK
            out[f, y] = grid[at : at + BLOCK]


def on_device(state_old):
    slices = lax.axis_size("tm")
    fields = state_old[0]
    held = [jnp.asarray(table) for table in tables()]
    inputs = [pltpu.with_memory_space_constraint(a, pltpu.HBM) for a in [fields] + held]
    half = pltpu.VMEM((4 * KY, 2 * N), jnp.float32)
    modes = pltpu.VMEM((PLANES, 4 * KY, 2 * N), jnp.float32)
    passing = [
        pltpu.VMEM((2 * slices * TILE, N), jnp.float32),
        pltpu.VMEM((2 * slices * TILE, N), jnp.float32),
        pltpu.SemaphoreType.DMA((2 * slices,)),
        pltpu.SemaphoreType.DMA((2 * slices,)),
        pltpu.SemaphoreType.DMA((2,)),
    ]
    last = exchange_scratch(PLANE_ROWS, GRID_ROWS)
    synth_rows = PLANES * GROUP * SYNTH_PACKS * THIN
    product_rows = PLANES * GROUP * PRODUCT_PACKS * THIN
    spectral = pltpu.VMEM((SPECTRAL_ROWS, N), jnp.float32)
    arrived = pl.pallas_call(
        whole_kernel,
        name="whole",
        out_shape=jax.ShapeDtypeStruct((GRID_ROWS, N), jnp.float32),
        in_specs=[pl.BlockSpec(memory_space=pltpu.HBM)] * len(inputs),
        out_specs=pl.BlockSpec(memory_space=pltpu.VMEM),
        scratch_shapes=[pltpu.VMEM(a.shape, a.dtype) for a in inputs]
        + [
            pltpu.SemaphoreType.DMA((BLOCK // STEP,)),
            pltpu.SemaphoreType.DMA((len(held),)),
        ]
        + exchange_scratch(GRID_ROWS, PLANE_ROWS)
        + exchange_scratch(synth_rows, synth_rows)
        + exchange_scratch(product_rows, product_rows)
        + [last[0]]
        + last[2:]
        + [spectral, spectral, spectral]
        + [
            pltpu.VMEM((2, 2 * N, 2 * N), jnp.float32),
            half,
            half,
            modes,
            modes,
            pltpu.VMEM((2, 4, COARSE_ROWS, N), jnp.float32),
            pltpu.VMEM((2, 16, 8, N), jnp.float32),
        ]
        + passing
        + passing,
        compiler_params=pltpu.CompilerParams(
            collective_id=0, has_side_effects=True, vmem_limit_bytes=VMEM_BYTES
        ),
    )(*inputs)
    result = pl.pallas_call(
        lines_kernel,
        name="lines",
        grid=(BLOCK // STEP,),
        out_shape=jax.ShapeDtypeStruct(fields.shape, jnp.float32),
        in_specs=[pl.BlockSpec(memory_space=pltpu.VMEM)] * 2,
        out_specs=pl.BlockSpec((4, STEP, BLOCK, N), lambda i: (0, i, 0, 0)),
        compiler_params=pltpu.CompilerParams(vmem_limit_bytes=16 << 20),
    )(arrived, held[1])
    return result[None]


def solution(mesh):
    return jax.shard_map(
        on_device,
        mesh=mesh,
        in_specs=(P("tm", None, "py", "pz", None),),
        out_specs=P("tm", None, "py", "pz", None),
        check_vma=False,
    )
```

```python
import functools

import jax
import jax.numpy as jnp
import numpy as np
from jax import lax
from jax.experimental import pallas as pl
from jax.experimental.pallas import tpu as pltpu
from jax.sharding import PartitionSpec as P

KMAX = 42
KCO = 21
N = 128
KY = 88
PLANES = 3
GROUP = 16
BLOCK = 32
MODE_ROWS = 88
HOLDERS = KMAX + 1 - 2 * GROUP
KZ = 2 * KMAX + 1
EMPTY = PLANES * GROUP - KMAX - 1
THIN = N // GROUP
SYNTH_PACKS = 6
PRODUCT_PACKS = 11
PITCH = BLOCK + 1
SPECTRAL_ROWS = 2 * PLANES * GROUP * PITCH
GRID_ROWS = MODE_ROWS * BLOCK
PLANE_ROWS = PLANES * GROUP * 2 * BLOCK
SCAN = 6
ORDER = (
    (2, 2), (2, 3), (1, 2), (3, 2), (1, 3), (3, 3), (2, 0), (2, 1),
    (0, 2), (0, 3), (1, 0), (3, 0), (1, 1), (3, 1), (0, 1),
)
MESH = pl.DeviceIdType.MESH
VMEM_BYTES = 50 << 20

time_step = 0.01
coriolis = 6.0
buoyancy_square = 100.0
viscosity = 0.001
diffusivity = 0.001


def halves(table):
    exact = np.asarray(table, np.float32)
    high = exact.astype(jnp.bfloat16)
    low = (exact - high.astype(np.float32)).astype(jnp.bfloat16)
    return high, low


def tables():
    scale = N**-0.5
    cells = np.arange(N)
    waves_x = np.arange(PLANES * GROUP)
    angle = 2 * np.pi / N * ((waves_x[:, None] * cells) % N)
    inside = (waves_x <= KMAX)[:, None] * scale
    fore = np.stack([np.cos(angle), -np.sin(angle)], axis=1) * inside[:, None]
    weight = np.where(waves_x == 0, 1.0, 2.0)[:, None, None]
    back = fore * weight
    rest = ((0, N - 2 * PLANES * GROUP), (0, 0))
    fore = np.pad(fore.reshape(-1, N), rest).T
    back = np.pad(back.reshape(-1, N), rest)

    def one_pass(table):
        high, low = halves(table)
        return np.concatenate(
            [
                np.concatenate([high, low], axis=1),
                np.concatenate([high, np.zeros_like(high)], axis=1),
            ]
        )

    def one_left(table):
        high, low = halves(table)
        return np.concatenate(
            [
                np.concatenate([high, high], axis=1),
                np.concatenate([low, np.zeros_like(low)], axis=1),
            ]
        )

    def pair(slots):
        waves = np.arange(slots) - KMAX
        angle = 2 * np.pi / N * ((waves[:, None] * cells[None, :]) % N)
        inside = (waves <= KMAX)[:, None] * scale
        return np.cos(angle) * inside, np.sin(angle) * inside

    cos_y, sin_y = pair(KY)
    cos_z, sin_z = pair(N)
    fore_y = np.block([[cos_y, sin_y], [-sin_y, cos_y]])
    back_y = np.block([[cos_y.T, -sin_y.T], [sin_y.T, cos_y.T]])
    fore_z = np.block([[cos_z.T, -sin_z.T], [sin_z.T, cos_z.T]])
    back_z = np.block([[cos_z, sin_z], [-sin_z, cos_z]])
    stack = lambda table: np.concatenate(halves(table))
    slots = 2 * PLANES * GROUP
    return (
        one_left(fore.T[:slots]),
        one_left(back[:slots].T),
        stack(fore_y),
        stack(back_y),
        stack(fore_z),
        stack(back_z),
        one_pass(back),
    )


def split(values):
    high = values.astype(jnp.bfloat16)
    low = (values - high.astype(jnp.float32)).astype(jnp.bfloat16)
    return high, low


def mul(left, right):
    return jnp.dot(left, right, preferred_element_type=jnp.float32)


def by_x(values, table):
    out = mul(jnp.concatenate(split(values), axis=1), table[...])
    return out[:, :N] + out[:, N:]


def by_left_once(table, values):
    rows = table.shape[0] // 2
    out = mul(table[...], jnp.concatenate(split(values)))
    return out[:rows] + out[rows:]


def by_turned(table, values):
    rows = table.shape[0] // 2
    turned = (((1,), (1,)), ((), ()))
    pair = jnp.concatenate(split(values), axis=1)
    out = lax.dot_general(table[...], pair, turned, preferred_element_type=jnp.float32)
    return out[:rows] + out[rows:]


def by_left(table, values):
    rows = table.shape[0] // 2
    high, low = split(values)
    out = mul(table[...], high)
    return out[:rows] + out[rows:] + mul(table[:rows], low)


def by_right(values, table):
    rows = table.shape[0] // 2
    high, low = split(values)
    return mul(high, table[:rows]) + mul(low, table[:rows]) + mul(high, table[rows:])


def swap_groups(parts):
    lane = lax.broadcasted_iota(jnp.int32, parts[0].shape, 1)
    low_half = lane < 64
    even = (lane // 32) % 2 == 0
    a0, a1, a2, a3 = parts
    p0 = jnp.where(low_half, a0, pltpu.roll(a2, 64, 1))
    p2 = jnp.where(low_half, pltpu.roll(a0, 64, 1), a2)
    p1 = jnp.where(low_half, a1, pltpu.roll(a3, 64, 1))
    p3 = jnp.where(low_half, pltpu.roll(a1, 64, 1), a3)
    return (
        jnp.where(even, p0, pltpu.roll(p1, 32, 1)),
        jnp.where(even, pltpu.roll(p0, 96, 1), p1),
        jnp.where(even, p2, pltpu.roll(p3, 32, 1)),
        jnp.where(even, pltpu.roll(p2, 96, 1), p3),
    )


def place():
    tm, py, pz = lax.axis_index("tm"), lax.axis_index("py"), lax.axis_index("pz")
    return tm, py, pz, py * 4 + pz


def rows_at(start, count):
    return pl.ds(pl.multiple_of(start, 8), count)


class Exchange:
    def __init__(self, refs, to_modes, rows):
        self.source, self.target, self.send, self.receive, self.own = refs
        self.to_modes, self.rows = to_modes, rows

    def chunk(self, owner, plane):
        return rows_at((plane * GROUP + owner) * self.rows, self.rows)

    def local(self, plane):
        _, _, _, me = place()
        part = self.chunk(me, plane)
        return pltpu.make_async_copy(
            self.source.at[part, :], self.target.at[part, :], self.own.at[plane]
        )

    def remote(self, step, plane):
        tm, py, pz, me = place()
        to_y, to_z = (py + step[0]) % 4, (pz + step[1]) % 4
        return pltpu.make_async_remote_copy(
            src_ref=self.source.at[self.chunk(to_y * 4 + to_z, plane), :],
            dst_ref=self.target.at[self.chunk(me, plane), :],
            send_sem=self.send.at[plane],
            recv_sem=self.receive.at[plane],
            device_id=(tm, to_y, to_z),
            device_id_type=MESH,
        )

    def amount(self, count, plane):
        tm, py, pz, _ = place()
        rows = pl.ds(0, count * self.rows)
        return pltpu.make_async_remote_copy(
            src_ref=self.source.at[rows, :],
            dst_ref=self.target.at[rows, :],
            send_sem=self.send.at[plane],
            recv_sem=self.receive.at[plane],
            device_id=(tm, (py + 1) % 4, pz),
            device_id_type=MESH,
        )

    def start(self, plane):
        _, py, pz, me = place()

        def go(step):
            to = (py + step[0]) % 4 * 4 + (pz + step[1]) % 4
            if not self.to_modes or (isinstance(plane, int) and plane < PLANES - 1):
                self.remote(step, plane).start()
            else:
                pl.when(to + GROUP * plane <= KMAX)(lambda: self.remote(step, plane).start())

        def all_steps():
            for step in ORDER:
                go(step)

        if self.to_modes:
            all_steps()

        @pl.when(me + GROUP * plane <= KMAX)
        def _():
            if not self.to_modes:
                all_steps()
            self.local(plane).start()

    def modes_side(self, plane, done):
        _, _, _, me = place()

        @pl.when(me + GROUP * plane <= KMAX)
        def _():
            done(self.amount(GROUP - 1, plane))

    def grid_side(self, plane, done):
        _, _, _, me = place()

        @pl.when(plane < PLANES - 1)
        def _():
            done(self.amount(GROUP - 1, plane))

        @pl.when((plane == PLANES - 1) & (me < HOLDERS))
        def _():
            done(self.amount(HOLDERS - 1, plane))

        @pl.when((plane == PLANES - 1) & (me >= HOLDERS))
        def _():
            done(self.amount(HOLDERS, plane))

    def arrived(self, plane):
        _, _, _, me = place()
        side = self.modes_side if self.to_modes else self.grid_side
        side(plane, lambda copy: copy.wait_recv())

        @pl.when(me + GROUP * plane <= KMAX)
        def _():
            self.local(plane).wait()

    def sent(self, plane):
        side = self.grid_side if self.to_modes else self.modes_side
        side(plane, lambda copy: copy.wait_send())


def exchange_scratch(source, target):
    return [
        pltpu.VMEM((source, N), jnp.float32),
        pltpu.VMEM((target, N), jnp.float32),
        pltpu.SemaphoreType.DMA((PLANES,)),
        pltpu.SemaphoreType.DMA((PLANES,)),
        pltpu.SemaphoreType.DMA((PLANES,)),
    ]


def load_fields_x(source, table, first, count):
    lines = []
    for y in range(count):
        rows = source[pl.ds(first + y, MODE_ROWS, stride=PITCH), :]
        rows = jnp.concatenate([rows, jnp.zeros((N - MODE_ROWS, N), jnp.float32)])
        lines.append(rows.T)
    return by_x(jnp.concatenate(lines), table)


def fore_plane(received, plane, planes, fore_y, fore_z):
    for part in range(2):
        for block in range(4):
            blocks = []
            for s in range(4):
                start = ((plane * GROUP + block * 4 + s) * 2 + part) * BLOCK
                blocks.append(received[pl.ds(pl.multiple_of(start, BLOCK), BLOCK), :])
            for f, piece in enumerate(swap_groups(blocks)):
                rows = pl.ds(part * N + block * BLOCK, BLOCK)
                planes[f // 2, rows, (f % 2) * N : (f % 2 + 1) * N] = piece
    lines = []
    for duo in range(2):
        along_y = by_left(fore_y, planes[duo])
        for f in range(2):
            own = along_y[:, f * N : (f + 1) * N]
            lines.append(jnp.concatenate([own[:KY], own[KY:]], axis=1))
    return by_right(jnp.concatenate(lines), fore_z)


def back_plane(modes, plane, target, back_y, back_z):
    along_z = by_right(modes, back_z)
    fields = []
    for duo in range(2):
        both = []
        for f in range(2):
            own = along_z[(2 * duo + f) * KY : (2 * duo + f + 1) * KY]
            both.append(jnp.concatenate([own[:, :N], own[:, N:]]))
        along_y = by_left(back_y, jnp.concatenate(both, axis=1))
        fields += [along_y[:, :N], along_y[:, N:]]
    for part in range(2):
        for block in range(4):
            rows = slice(part * N + block * BLOCK, part * N + (block + 1) * BLOCK)
            for s, piece in enumerate(swap_groups([field[rows] for field in fields])):
                start = ((plane * GROUP + block * 4 + s) * 2 + part) * BLOCK
                target[pl.ds(pl.multiple_of(start, BLOCK), BLOCK), :] = piece


def pack(pieces):
    out = []
    whole = len(pieces) // 3 * 3
    for first in range(0, whole, 3):
        one, two, three = pieces[first : first + 3]
        lane = lax.broadcasted_iota(jnp.int32, one.shape, 1)
        turned = pltpu.roll(two, KZ, 1)
        out.append(jnp.where(lane < KZ, one, turned))
        out.append(jnp.where(lane < 2 * KZ - N, turned, pltpu.roll(three, 2 * KZ - N, 1)))
    return out + list(pieces[whole:])


def unpack(packs, count):
    out = []
    for first in range(0, count // 3 * 2, 2):
        one, two = packs[first : first + 2]
        lane = lax.broadcasted_iota(jnp.int32, one.shape, 1)
        out.append(one)
        out.append(pltpu.roll(jnp.where(lane < 2 * KZ - N, two, one), N - KZ, 1))
        out.append(pltpu.roll(two, 2 * N - 2 * KZ, 1))
    return out + list(packs[count // 3 * 2 :])


def beside(left, right):
    return jnp.concatenate([left, right], axis=1)


def spread_packs(packs, plane, target):
    for owner in range(GROUP):
        for k, values in enumerate(packs):
            start = ((plane * GROUP + owner) * len(packs) + k) * THIN
            target[rows_at(start, THIN), :] = values[owner * THIN : (owner + 1) * THIN]


def gather_packs(source, plane, count):
    packs = []
    for k in range(count):
        starts = [((plane * GROUP + owner) * count + k) * THIN for owner in range(GROUP)]
        packs.append(jnp.concatenate([source[rows_at(at, THIN), :] for at in starts]))
    return packs


def back_along_y(values, plane, target, back_y):
    pieces = []
    for duo in range(2):
        both = []
        for f in (2 * duo, 2 * duo + 1):
            own = values[f * KY : (f + 1) * KY]
            both.append(jnp.concatenate([own[:, :N], own[:, N:]]))
        along = by_left(back_y, beside(*both))
        pieces += [along[:N, :N], along[N:, :N], along[:N, N:], along[N:, N:]]
    spread_packs(pack(pieces), plane, target)


def back_along_z(source, plane, spectral, back_z):
    pieces = unpack(gather_packs(source, plane, SYNTH_PACKS), 8)
    lines = [beside(pieces[2 * f], pieces[2 * f + 1]) for f in range(4)]
    along = by_right(jnp.concatenate(lines), back_z)
    for owner in range(GROUP):
        for f in range(4):
            rows = slice(f * N + owner * THIN, f * N + (owner + 1) * THIN)
            for c in range(2):
                start = ((plane * GROUP + owner) * 2 + c) * PITCH + f * THIN
                spectral[pl.ds(start, THIN), :] = along[rows, c * N : (c + 1) * N]


def fore_along_z(spectral, plane, target, fore_z):
    pieces = []
    for ref in spectral:
        lines = []
        for owner in range(GROUP):
            start = (plane * GROUP + owner) * 2 * PITCH
            both = [ref[pl.ds(start + c * PITCH, BLOCK), :] for c in range(2)]
            lines.append(beside(*both))
        along = by_right(jnp.concatenate(lines), fore_z)
        for f in range(4):
            for c in range(2):
                pieces.append(
                    jnp.concatenate(
                        [
                            along[
                                owner * BLOCK + f * THIN : owner * BLOCK + (f + 1) * THIN,
                                c * N : (c + 1) * N,
                            ]
                            for owner in range(GROUP)
                        ]
                    )
                )
    spread_packs(pack(pieces), plane, target)


def fore_along_y(source, plane, modes, fore_y):
    pieces = unpack(gather_packs(source, plane, PRODUCT_PACKS), 16)
    for duo in range(4):
        both = [
            jnp.concatenate([pieces[2 * f], pieces[2 * f + 1]])
            for f in (2 * duo, 2 * duo + 1)
        ]
        along = by_left(fore_y, beside(*both))
        ref = modes[duo // 2]
        for half in range(2):
            rows = slice((duo % 2 * 2 + half) * KY, (duo % 2 * 2 + half + 1) * KY)
            own = along[:, half * N : (half + 1) * N]
            ref[rows, :N] = own[:KY]
            ref[rows, N:] = own[KY:]


def waves_at(plane):
    _, _, _, me = place()
    wave_x = (me + GROUP * plane).astype(jnp.float32)
    wave_y = (lax.broadcasted_iota(jnp.int32, (KY, N), 0) - KMAX).astype(jnp.float32)
    wave_z = (lax.broadcasted_iota(jnp.int32, (KY, N), 1) - KMAX).astype(jnp.float32)
    return wave_x, wave_y, wave_z


def squared(waves):
    wave_x, wave_y, wave_z = waves
    return wave_x * wave_x + wave_y * wave_y + wave_z * wave_z


def project(velocity, waves, inverse):
    wave_x, wave_y, wave_z = waves
    along = (wave_x * velocity[0] + wave_y * velocity[1] + wave_z * velocity[2]) * inverse
    return (
        velocity[0] - wave_x * along,
        velocity[1] - wave_y * along,
        velocity[2] - wave_z * along,
    )


def linear(state, waves, square, inverse):
    pushed = project((coriolis * state[1], -coriolis * state[0], state[3]), waves, inverse)
    return (
        pushed[0] - viscosity * square * state[0],
        pushed[1] - viscosity * square * state[1],
        pushed[2] - viscosity * square * state[2],
        -buoyancy_square * state[2] - diffusivity * square * state[3],
    )


def propagate(state, waves):
    square = squared(waves)
    inverse = 1.0 / jnp.maximum(square, 1.0)
    for half_step in range(2):
        anchor = state
        for order in (4.0, 3.0, 2.0, 1.0):
            rate = linear(state, waves, square, inverse)
            state = tuple(a + (0.5 * time_step / order) * r for a, r in zip(anchor, rate))
    return state


FIRST_ROW = 16
COARSE_ROWS = 8 * SCAN
TILE = 8 * 4
STEP = 4
LINES = 16


def coarse_waves(plane, row0, rows):
    _, _, _, me = place()
    row = lax.broadcasted_iota(jnp.int32, (rows, N), 0) + row0
    lane = lax.broadcasted_iota(jnp.int32, (rows, N), 1) % 64
    wave_x = (me + GROUP * plane).astype(jnp.float32)
    wave_y = (row - KMAX).astype(jnp.float32)
    wave_z = (lane - KMAX).astype(jnp.float32)
    return wave_x, wave_y, wave_z


def coarse_inside(waves):
    wave_x, wave_y, wave_z = waves
    inside = (jnp.abs(wave_y) <= KCO) & (jnp.abs(wave_z) <= KCO)
    return inside & jnp.broadcast_to(wave_x <= KCO, inside.shape)


def packed(ref, plane, f):
    rows = pl.ds(f * KY + FIRST_ROW, COARSE_ROWS)
    lane = lax.broadcasted_iota(jnp.int32, (COARSE_ROWS, N), 1)
    real, imag = ref[plane, rows, :N], ref[plane, rows, N:]
    return jnp.where(lane < 64, real, pltpu.roll(imag, 64, 1))


class Passing:
    def __init__(self, refs):
        self.source, self.target, self.send, self.receive, self.own = refs

    def rows(self, owner, plane):
        slices = lax.axis_size("tm")
        return pl.ds(pl.multiple_of((plane * slices + owner) * TILE, TILE), TILE)

    def remote(self, i, plane, origin):
        tm, py, pz, _ = place()
        slices = lax.axis_size("tm")
        to = (tm + i) % slices
        where = (tm + slices - i) % slices if origin else tm
        return pltpu.make_async_remote_copy(
            src_ref=self.source.at[self.rows(to, plane), :],
            dst_ref=self.target.at[self.rows(where, plane), :],
            send_sem=self.send.at[plane * slices + i],
            recv_sem=self.receive.at[plane * slices + i],
            device_id=(to, py, pz),
            device_id_type=MESH,
        )

    def local(self, plane):
        tm, _, _, _ = place()
        part = self.rows(tm, plane)
        return pltpu.make_async_copy(
            self.source.at[part, :], self.target.at[part, :], self.own.at[plane]
        )


def whole_kernel(
    fields_hbm, fore_x_hbm, back_x_hbm, fore_y_hbm, back_y_hbm, fore_z_hbm, back_z_hbm,
    into4,
    fields, fore_x, back_x, fore_y, back_y, fore_z, back_z,
    load_sem, table_sem,
    out0, into0, send0, receive0, own0,
    out1, into1, send1, receive1, own1,
    out2, into2, send2, receive2, own2,
    out4, send4, receive4, own4,
    synth, first_products, second_products,
    planes, first_modes, second_modes, start, fine, moved, matrix,
    coarse_out, coarse_in, coarse_send, coarse_receive, coarse_own,
    carry_out, carry_in, carry_send, carry_receive, carry_own,
):
    tm, py, pz, me = place()
    slices = lax.axis_size("tm")
    empty = jnp.zeros((2 * BLOCK, N), jnp.float32)
    into1[pl.ds((KMAX + 1) * SYNTH_PACKS * THIN, EMPTY * SYNTH_PACKS * THIN), :] = jnp.zeros(
        (EMPTY * SYNTH_PACKS * THIN, N), jnp.float32
    )
    into4[pl.ds(GRID_ROWS - 2 * BLOCK, 2 * BLOCK), :] = empty
    coarse_in[...] = jnp.zeros_like(coarse_in)
    barrier = pltpu.get_barrier_semaphore()

    def greet(i, carry):
        peer = (tm, (py + i // 4) % 4, (pz + i % 4) % 4)
        pl.semaphore_signal(barrier, inc=1, device_id=peer, device_id_type=MESH)
        return carry

    lax.fori_loop(1, GROUP, greet, 0)

    def greet_slices(i, carry):
        peer = ((tm + i) % slices, py, pz)
        pl.semaphore_signal(barrier, inc=1, device_id=peer, device_id_type=MESH)
        return carry

    lax.fori_loop(1, slices, greet_slices, 0)

    loads = [
        pltpu.make_async_copy(held, ref, table_sem.at[i])
        for i, (held, ref) in enumerate(
            [
                (fore_x_hbm, fore_x),
                (fore_y_hbm, fore_y),
                (fore_z_hbm, fore_z),
                (back_z_hbm, back_z),
                (back_y_hbm, back_y),
                (back_x_hbm, back_x),
            ]
        )
    ]
    loads[0].start()

    def field_load(step):
        lines = pl.ds(pl.multiple_of(step * STEP, STEP), STEP)
        return pltpu.make_async_copy(
            fields_hbm.at[:, lines], fields.at[:, lines], load_sem.at[step]
        )

    def load(step, carry):
        field_load(step).start()
        return carry

    lax.fori_loop(0, BLOCK // STEP, load, 0)
    for copy in loads[1:]:
        copy.start()
    loads[0].wait()

    analysed = Exchange((out0, into0, send0, receive0, own0), True, 2 * BLOCK)
    to_grid = Exchange((out1, into1, send1, receive1, own1), False, SYNTH_PACKS * THIN)
    to_modes = Exchange((out2, into2, send2, receive2, own2), True, PRODUCT_PACKS * THIN)
    final = Exchange((out4, into4, send4, receive4, own4), False, 2 * BLOCK)
    coarse = Passing((coarse_out, coarse_in, coarse_send, coarse_receive, coarse_own))
    back = Passing((carry_out, carry_in, carry_send, carry_receive, carry_own))
    coarse_second = me + GROUP <= KCO

    def has_coarse(plane):
        return me + GROUP * plane <= KCO

    def analyse(step, carry):
        first = step * STEP
        field_load(step).wait()
        for duo in range(STEP // 2):
            rows = [fields[f, first + 2 * duo + y] for y in range(2) for f in range(4)]
            modes = by_turned(fore_x, jnp.concatenate(rows))
            for y in range(2):
                own = modes[:MODE_ROWS, y * N : (y + 1) * N]
                synth[pl.ds(first + 2 * duo + y, MODE_ROWS, stride=PITCH), :] = own
        return carry

    lax.fori_loop(0, BLOCK // STEP, analyse, 0)
    for slot in range(MODE_ROWS):
        out0[pl.ds(slot * BLOCK, BLOCK), :] = synth[pl.ds(slot * PITCH, BLOCK), :]
    pl.semaphore_wait(barrier, GROUP - 1 + slices - 1)
    for plane in range(PLANES):
        analysed.start(plane)
    for copy in loads[1:]:
        copy.wait()

    def first_pass(plane, carry):
        analysed.arrived(plane)

        @pl.when(me + GROUP * plane <= KMAX)
        def _():
            first_modes[...] = fore_plane(into0, plane, planes, fore_y, fore_z)
            waves = waves_at(plane)
            inverse = 1.0 / jnp.maximum(squared(waves), 1.0)
            for part in range(2):
                lanes = slice(part * N, (part + 1) * N)
                state = [first_modes[f * KY : (f + 1) * KY, lanes] for f in range(4)]
                for f, value in enumerate(project(state[:3], waves, inverse) + (state[3],)):
                    start[plane, pl.ds(f * KY, KY), lanes] = value
            back_along_y(start[plane], plane, out1, back_y)
            to_grid.start(plane)

        return carry

    lax.fori_loop(0, PLANES, first_pass, 0)

    def move(plane, carry):
        @pl.when(has_coarse(plane) & (tm > 0))
        def _():
            waves = coarse_waves(plane, FIRST_ROW, COARSE_ROWS)
            before = tuple(packed(start, plane, f) for f in range(4))
            for f, value in enumerate(propagate(before, waves)):
                moved[plane, f] = value

        @pl.when(has_coarse(plane) & (tm == 0))
        def _():
            moved[plane] = jnp.zeros((4, COARSE_ROWS, N), jnp.float32)

        waves = coarse_waves(plane, FIRST_ROW + tm * 8, 8)
        keep = coarse_inside(waves).astype(jnp.float32)
        zero = jnp.zeros((8, N), jnp.float32)
        for f in range(4):
            unit = tuple(zero + (1.0 if g == f else 0.0) for g in range(4))
            for g, value in enumerate(propagate(unit, waves)):
                matrix[plane, g * 4 + f] = keep * value
        return carry

    lax.fori_loop(0, 2, move, 0)

    def gather(plane, carry):
        to_grid.arrived(plane)
        back_along_z(into1, plane, synth, back_z)
        return carry

    lax.fori_loop(0, PLANES, gather, 0)

    def lines(y, carry):
        slots = 2 * PLANES * GROUP

        def modes_at(ref, f):
            return ref.at[pl.ds(y + f * THIN, slots, stride=PITCH), :]

        grid = []
        for f in (0, 2):
            both = beside(modes_at(synth, f)[...], modes_at(synth, f + 1)[...])
            both = by_left_once(back_x, both)
            grid += [both[:, :N], both[:, N:]]
        u, v, w, b = grid
        rest = w * w
        one = [u * u - rest, v * v - rest, u * v, u * w]
        two = [v * w, u * b, v * b, w * b]
        for ref, values in ((first_products, one), (second_products, two)):
            for f in (0, 2):
                both = by_left_once(fore_x, beside(values[f], values[f + 1]))
                modes_at(ref, f)[...] = both[:, :N]
                modes_at(ref, f + 1)[...] = both[:, N:]
        return carry

    lax.fori_loop(0, THIN, lines, 0)

    def scatter(plane, carry):
        fore_along_z((first_products, second_products), plane, out2, fore_z)
        to_modes.start(plane)
        return carry

    lax.fori_loop(0, PLANES, scatter, 0)

    def second_pass(plane, carry):
        to_modes.arrived(plane)

        @pl.when(me + GROUP * plane <= KMAX)
        def _():
            fore_along_y(into2, plane, (first_modes, second_modes), fore_y)
            waves = waves_at(plane)
            wave_x, wave_y, wave_z = waves
            square = squared(waves)
            inverse = 1.0 / jnp.maximum(square, 1.0)
            for part in range(2):
                lanes = slice(part * N, (part + 1) * N)
                other = slice((1 - part) * N, (2 - part) * N)
                sign = 1.0 if part == 0 else -1.0
                xx, yy, xy, xz = (first_modes[f * KY : (f + 1) * KY, other] for f in range(4))
                yz, bx, by, bz = (second_modes[f * KY : (f + 1) * KY, other] for f in range(4))
                state = [start[plane, pl.ds(f * KY, KY), lanes] for f in range(4)]
                change = (
                    sign * (wave_x * xx + wave_y * xy + wave_z * xz),
                    sign * (wave_x * xy + wave_y * yy + wave_z * yz),
                    sign * (wave_x * xz + wave_y * yz),
                )
                lifted = sign * (wave_x * bx + wave_y * by + wave_z * bz)
                pushed = project(
                    (
                        change[0] + coriolis * state[1],
                        change[1] - coriolis * state[0],
                        change[2] + state[3],
                    ),
                    waves,
                    inverse,
                )
                rates = [pushed[f] - viscosity * square * state[f] for f in range(3)]
                rates.append(
                    lifted - buoyancy_square * state[2] - diffusivity * square * state[3]
                )
                for f in range(4):
                    fine[plane, pl.ds(f * KY, KY), lanes] = state[f] + time_step * rates[f]

        @pl.when(has_coarse(plane))
        def _():
            waves = coarse_waves(plane, FIRST_ROW, COARSE_ROWS)
            keep = coarse_inside(waves).astype(jnp.float32)
            for f in range(4):
                here = keep * packed(fine, plane, f) - keep * moved[plane, f]
                for tile in range(SCAN):
                    at = pl.multiple_of((plane * slices + tile) * TILE + f * 8, 8)
                    coarse_out[pl.ds(at, 8), :] = here[tile * 8 : tile * 8 + 8]

            def go(i, carry):
                @pl.when((tm + i) % slices < SCAN)
                def _():
                    coarse.remote(i, plane, False).start()

                return carry

            lax.fori_loop(1, slices, go, 0)

            @pl.when(tm < SCAN)
            def _():
                coarse.local(plane).start()

        @pl.when((plane == 1) & (tm < SCAN))
        def _():
            def wait(which):
                def go(i, carry):
                    coarse.remote(i, which, True).wait_recv()
                    return carry

                lax.fori_loop(1, slices, go, 0)
                coarse.local(which).wait()

            wait(0)

            @pl.when(coarse_second)
            def _():
                wait(1)

            def rows(n, which, f):
                return pl.ds(pl.multiple_of((which * slices + n) * TILE + f * 8, 8), 8)

            def step(n, state):
                new = []
                for which in range(2):
                    held = state[which * 4 : which * 4 + 4]
                    for g in range(4):
                        value = coarse_in[rows(n, which, g), :]
                        for f in range(4):
                            value = value + matrix[which, g * 4 + f] * held[f]
                        carry_out[rows(n, which, g), :] = value
                        new.append(value)
                return tuple(new)

            lax.fori_loop(0, slices, step, tuple([jnp.zeros((8, N), jnp.float32)] * 8))

            def send(which):
                def go(i, carry):
                    back.remote(i, which, False).start()
                    return carry

                lax.fori_loop(1, slices, go, 0)
                back.local(which).start()

            send(0)

            @pl.when(coarse_second)
            def _():
                send(1)

        return carry

    lax.fori_loop(0, PLANES, second_pass, 0)

    def last_pass(step, carry):
        plane = PLANES - 1 - step

        @pl.when(me + GROUP * plane <= KMAX)
        def _():
            @pl.when((plane < 2) & has_coarse(plane))
            def _():
                def wait(i, carry):
                    @pl.when((tm + slices - i) % slices < SCAN)
                    def _():
                        back.remote(i, plane, True).wait_recv()

                    return carry

                lax.fori_loop(1, slices, wait, 0)

                @pl.when(tm < SCAN)
                def _():
                    back.local(plane).wait()

                waves = coarse_waves(plane, FIRST_ROW, COARSE_ROWS)
                lane = lax.broadcasted_iota(jnp.int32, (COARSE_ROWS, N), 1)
                here = coarse_inside(waves) & (lane < 64)
                for f in range(4):
                    tiles = []
                    for tile in range(SCAN):
                        at = pl.multiple_of((plane * slices + tile) * TILE + f * 8, 8)
                        tiles.append(carry_in[pl.ds(at, 8), :])
                    value = jnp.concatenate(tiles)
                    rows = pl.ds(f * KY + FIRST_ROW, COARSE_ROWS)
                    fine[plane, rows, :N] = jnp.where(here, value, fine[plane, rows, :N])
                    fine[plane, rows, N:] = jnp.where(
                        here, pltpu.roll(value, 64, 1), fine[plane, rows, N:]
                    )

            back_plane(fine[plane], plane, out4, back_y, back_z)
            final.start(plane)

        return carry

    lax.fori_loop(0, PLANES, last_pass, 0)

    def done(plane, carry):
        analysed.sent(plane)
        to_grid.sent(plane)
        to_modes.sent(plane)
        final.sent(plane)
        final.arrived(plane)
        return carry

    lax.fori_loop(0, PLANES, done, 0)

    def passed(q, carry):
        plane, i = q // slices, q % slices

        @pl.when((i > 0) & has_coarse(plane))
        def _():
            @pl.when((tm + i) % slices < SCAN)
            def _():
                coarse.remote(i, plane, False).wait_send()

            @pl.when(tm < SCAN)
            def _():
                back.remote(i, plane, False).wait_send()

        return carry

    lax.fori_loop(0, 2 * slices, passed, 0)


def lines_kernel(modes, back_x, out, held):
    @pl.when(pl.program_id(0) == 0)
    def _():
        for slot in range(MODE_ROWS):
            held[pl.ds(slot * PITCH, BLOCK), :] = modes[pl.ds(slot * BLOCK, BLOCK), :]

    grid = load_fields_x(held, back_x, pl.program_id(0) * LINES, LINES)
    for y in range(LINES):
        for f in range(4):
            at = y * N + f * BLOCK
            out[f, y] = grid[at : at + BLOCK]


def on_device(state_old):
    slices = lax.axis_size("tm")
    fields = state_old[0]
    held = [jnp.asarray(table) for table in tables()]
    inner = held[:-1]
    inputs = [pltpu.with_memory_space_constraint(a, pltpu.HBM) for a in [fields] + inner]
    half = pltpu.VMEM((4 * KY, 2 * N), jnp.float32)
    modes = pltpu.VMEM((PLANES, 4 * KY, 2 * N), jnp.float32)
    passing = [
        pltpu.VMEM((2 * slices * TILE, N), jnp.float32),
        pltpu.VMEM((2 * slices * TILE, N), jnp.float32),
        pltpu.SemaphoreType.DMA((2 * slices,)),
        pltpu.SemaphoreType.DMA((2 * slices,)),
        pltpu.SemaphoreType.DMA((2,)),
    ]
    last = exchange_scratch(PLANE_ROWS, GRID_ROWS)
    synth_rows = PLANES * GROUP * SYNTH_PACKS * THIN
    product_rows = PLANES * GROUP * PRODUCT_PACKS * THIN
    spectral = pltpu.VMEM((SPECTRAL_ROWS, N), jnp.float32)
    arrived = pl.pallas_call(
        whole_kernel,
        name="whole",
        out_shape=jax.ShapeDtypeStruct((GRID_ROWS, N), jnp.float32),
        in_specs=[pl.BlockSpec(memory_space=pltpu.HBM)] * len(inputs),
        out_specs=pl.BlockSpec(memory_space=pltpu.VMEM),
        scratch_shapes=[pltpu.VMEM(a.shape, a.dtype) for a in inputs]
        + [
            pltpu.SemaphoreType.DMA((BLOCK // STEP,)),
            pltpu.SemaphoreType.DMA((len(inner),)),
        ]
        + exchange_scratch(GRID_ROWS, PLANE_ROWS)
        + exchange_scratch(synth_rows, synth_rows)
        + exchange_scratch(product_rows, product_rows)
        + [last[0]]
        + last[2:]
        + [spectral, spectral, spectral]
        + [
            pltpu.VMEM((2, 2 * N, 2 * N), jnp.float32),
            half,
            half,
            modes,
            modes,
            pltpu.VMEM((2, 4, COARSE_ROWS, N), jnp.float32),
            pltpu.VMEM((2, 16, 8, N), jnp.float32),
        ]
        + passing
        + passing,
        compiler_params=pltpu.CompilerParams(
            collective_id=0, has_side_effects=True, vmem_limit_bytes=VMEM_BYTES
        ),
    )(*inputs)
    result = pl.pallas_call(
        lines_kernel,
        name="lines",
        grid=(BLOCK // LINES,),
        out_shape=jax.ShapeDtypeStruct(fields.shape, jnp.float32),
        in_specs=[pl.BlockSpec(memory_space=pltpu.VMEM)] * 2,
        scratch_shapes=[pltpu.VMEM((MODE_ROWS * PITCH, N), jnp.float32)],
        out_specs=pl.BlockSpec((4, LINES, BLOCK, N), lambda i: (0, i, 0, 0)),
        compiler_params=pltpu.CompilerParams(vmem_limit_bytes=16 << 20),
    )(arrived, held[-1])
    return result[None]


def solution(mesh):
    return jax.shard_map(
        on_device,
        mesh=mesh,
        in_specs=(P("tm", None, "py", "pz", None),),
        out_specs=P("tm", None, "py", "pz", None),
        check_vma=False,
    )
```

```python
import functools

import jax
import jax.numpy as jnp
import numpy as np
from jax import lax
from jax.experimental import pallas as pl
from jax.experimental.pallas import tpu as pltpu
from jax.sharding import PartitionSpec as P

KMAX = 42
KCO = 21
N = 128
KY = 88
PLANES = 3
GROUP = 16
BLOCK = 32
MODE_ROWS = 88
HOLDERS = KMAX + 1 - 2 * GROUP
KZ = 2 * KMAX + 1
EMPTY = PLANES * GROUP - KMAX - 1
THIN = N // GROUP
SYNTH_PACKS = 6
PRODUCT_PACKS = 11
PITCH = BLOCK + 1
SPECTRAL_ROWS = 2 * PLANES * GROUP * PITCH
GRID_ROWS = MODE_ROWS * BLOCK
PLANE_ROWS = PLANES * GROUP * 2 * BLOCK
SCAN = 6
ORDER = (
    (2, 2), (2, 3), (1, 2), (3, 2), (1, 3), (3, 3), (2, 0), (2, 1),
    (0, 2), (0, 3), (1, 0), (3, 0), (1, 1), (3, 1), (0, 1),
)
MESH = pl.DeviceIdType.MESH
VMEM_BYTES = 50 << 20

time_step = 0.01
coriolis = 6.0
buoyancy_square = 100.0
viscosity = 0.001
diffusivity = 0.001


def halves(table):
    exact = np.asarray(table, np.float32)
    high = exact.astype(jnp.bfloat16)
    low = (exact - high.astype(np.float32)).astype(jnp.bfloat16)
    return high, low


def tables():
    scale = N**-0.5
    cells = np.arange(N)
    waves_x = np.arange(PLANES * GROUP)
    angle = 2 * np.pi / N * ((waves_x[:, None] * cells) % N)
    inside = (waves_x <= KMAX)[:, None] * scale
    fore = np.stack([np.cos(angle), -np.sin(angle)], axis=1) * inside[:, None]
    weight = np.where(waves_x == 0, 1.0, 2.0)[:, None, None]
    back = fore * weight
    rest = ((0, N - 2 * PLANES * GROUP), (0, 0))
    fore = np.pad(fore.reshape(-1, N), rest).T
    back = np.pad(back.reshape(-1, N), rest)

    def one_pass(table):
        high, low = halves(table)
        return np.concatenate(
            [
                np.concatenate([high, low], axis=1),
                np.concatenate([high, np.zeros_like(high)], axis=1),
            ]
        )

    def one_left(table):
        high, low = halves(table)
        return np.concatenate(
            [
                np.concatenate([high, high], axis=1),
                np.concatenate([low, np.zeros_like(low)], axis=1),
            ]
        )

    def pair(slots):
        waves = np.arange(slots) - KMAX
        angle = 2 * np.pi / N * ((waves[:, None] * cells[None, :]) % N)
        inside = (waves <= KMAX)[:, None] * scale
        return np.cos(angle) * inside, np.sin(angle) * inside

    cos_y, sin_y = pair(KY)
    cos_z, sin_z = pair(N)
    fore_y = np.block([[cos_y, sin_y], [-sin_y, cos_y]])
    back_y = np.block([[cos_y.T, -sin_y.T], [sin_y.T, cos_y.T]])
    fore_z = np.block([[cos_z.T, -sin_z.T], [sin_z.T, cos_z.T]])
    back_z = np.block([[cos_z, sin_z], [-sin_z, cos_z]])
    stack = lambda table: np.concatenate(halves(table))
    slots = 2 * PLANES * GROUP
    return (
        one_left(fore.T[:slots]),
        one_left(back[:slots].T),
        stack(fore_y),
        stack(back_y),
        stack(fore_z),
        stack(back_z),
        one_pass(back),
    )


def split(values):
    high = values.astype(jnp.bfloat16)
    low = (values - high.astype(jnp.float32)).astype(jnp.bfloat16)
    return high, low


def mul(left, right):
    return jnp.dot(left, right, preferred_element_type=jnp.float32)


def by_x(values, table):
    out = mul(jnp.concatenate(split(values), axis=1), table[...])
    return out[:, :N] + out[:, N:]


def by_left_once(table, values):
    rows = table.shape[0] // 2
    out = mul(table[...], jnp.concatenate(split(values)))
    return out[:rows] + out[rows:]


def by_turned(table, values):
    rows = table.shape[0] // 2
    turned = (((1,), (1,)), ((), ()))
    pair = jnp.concatenate(split(values), axis=1)
    out = lax.dot_general(table[...], pair, turned, preferred_element_type=jnp.float32)
    return out[:rows] + out[rows:]


def by_left(table, values):
    rows = table.shape[0] // 2
    high, low = split(values)
    out = mul(table[...], high)
    return out[:rows] + out[rows:] + mul(table[:rows], low)


def by_right(values, table):
    rows = table.shape[0] // 2
    high, low = split(values)
    return mul(high, table[:rows]) + mul(low, table[:rows]) + mul(high, table[rows:])


def swap_groups(parts):
    lane = lax.broadcasted_iota(jnp.int32, parts[0].shape, 1)
    low_half = lane < 64
    even = (lane // 32) % 2 == 0
    a0, a1, a2, a3 = parts
    p0 = jnp.where(low_half, a0, pltpu.roll(a2, 64, 1))
    p2 = jnp.where(low_half, pltpu.roll(a0, 64, 1), a2)
    p1 = jnp.where(low_half, a1, pltpu.roll(a3, 64, 1))
    p3 = jnp.where(low_half, pltpu.roll(a1, 64, 1), a3)
    return (
        jnp.where(even, p0, pltpu.roll(p1, 32, 1)),
        jnp.where(even, pltpu.roll(p0, 96, 1), p1),
        jnp.where(even, p2, pltpu.roll(p3, 32, 1)),
        jnp.where(even, pltpu.roll(p2, 96, 1), p3),
    )


def place():
    tm, py, pz = lax.axis_index("tm"), lax.axis_index("py"), lax.axis_index("pz")
    return tm, py, pz, py * 4 + pz


def rows_at(start, count):
    return pl.ds(pl.multiple_of(start, 8), count)


class Exchange:
    def __init__(self, refs, to_modes, rows):
        self.source, self.target, self.send, self.receive, self.own = refs
        self.to_modes, self.rows = to_modes, rows

    def chunk(self, owner, plane):
        return rows_at((plane * GROUP + owner) * self.rows, self.rows)

    def local(self, plane):
        _, _, _, me = place()
        part = self.chunk(me, plane)
        return pltpu.make_async_copy(
            self.source.at[part, :], self.target.at[part, :], self.own.at[plane]
        )

    def remote(self, step, plane):
        tm, py, pz, me = place()
        to_y, to_z = (py + step[0]) % 4, (pz + step[1]) % 4
        return pltpu.make_async_remote_copy(
            src_ref=self.source.at[self.chunk(to_y * 4 + to_z, plane), :],
            dst_ref=self.target.at[self.chunk(me, plane), :],
            send_sem=self.send.at[plane],
            recv_sem=self.receive.at[plane],
            device_id=(tm, to_y, to_z),
            device_id_type=MESH,
        )

    def amount(self, count, plane):
        tm, py, pz, _ = place()
        rows = pl.ds(0, count * self.rows)
        return pltpu.make_async_remote_copy(
            src_ref=self.source.at[rows, :],
            dst_ref=self.target.at[rows, :],
            send_sem=self.send.at[plane],
            recv_sem=self.receive.at[plane],
            device_id=(tm, (py + 1) % 4, pz),
            device_id_type=MESH,
        )

    def start(self, plane):
        _, py, pz, me = place()

        def go(step):
            to = (py + step[0]) % 4 * 4 + (pz + step[1]) % 4
            if not self.to_modes or (isinstance(plane, int) and plane < PLANES - 1):
                self.remote(step, plane).start()
            else:
                pl.when(to + GROUP * plane <= KMAX)(lambda: self.remote(step, plane).start())

        def all_steps():
            for step in ORDER:
                go(step)

        if self.to_modes:
            all_steps()

        @pl.when(me + GROUP * plane <= KMAX)
        def _():
            if not self.to_modes:
                all_steps()
            self.local(plane).start()

    def modes_side(self, plane, done):
        _, _, _, me = place()

        @pl.when(me + GROUP * plane <= KMAX)
        def _():
            done(self.amount(GROUP - 1, plane))

    def grid_side(self, plane, done):
        _, _, _, me = place()

        @pl.when(plane < PLANES - 1)
        def _():
            done(self.amount(GROUP - 1, plane))

        @pl.when((plane == PLANES - 1) & (me < HOLDERS))
        def _():
            done(self.amount(HOLDERS - 1, plane))

        @pl.when((plane == PLANES - 1) & (me >= HOLDERS))
        def _():
            done(self.amount(HOLDERS, plane))

    def arrived(self, plane):
        _, _, _, me = place()
        side = self.modes_side if self.to_modes else self.grid_side
        side(plane, lambda copy: copy.wait_recv())

        @pl.when(me + GROUP * plane <= KMAX)
        def _():
            self.local(plane).wait()

    def sent(self, plane):
        side = self.grid_side if self.to_modes else self.modes_side
        side(plane, lambda copy: copy.wait_send())


def exchange_scratch(source, target):
    return [
        pltpu.VMEM((source, N), jnp.float32),
        pltpu.VMEM((target, N), jnp.float32),
        pltpu.SemaphoreType.DMA((PLANES,)),
        pltpu.SemaphoreType.DMA((PLANES,)),
        pltpu.SemaphoreType.DMA((PLANES,)),
    ]


def load_fields_x(source, table, first, count):
    lines = []
    for y in range(count):
        rows = source[pl.ds(first + y, MODE_ROWS, stride=PITCH), :]
        rows = jnp.concatenate([rows, jnp.zeros((N - MODE_ROWS, N), jnp.float32)])
        lines.append(rows.T)
    return by_x(jnp.concatenate(lines), table)


def fore_plane(received, plane, planes, fore_y, fore_z):
    for part in range(2):
        for block in range(4):
            blocks = []
            for s in range(4):
                start = ((plane * GROUP + block * 4 + s) * 2 + part) * BLOCK
                blocks.append(received[pl.ds(pl.multiple_of(start, BLOCK), BLOCK), :])
            for f, piece in enumerate(swap_groups(blocks)):
                rows = pl.ds(part * N + block * BLOCK, BLOCK)
                planes[f // 2, rows, (f % 2) * N : (f % 2 + 1) * N] = piece
    lines = []
    for duo in range(2):
        along_y = by_left(fore_y, planes[duo])
        for f in range(2):
            own = along_y[:, f * N : (f + 1) * N]
            lines.append(jnp.concatenate([own[:KY], own[KY:]], axis=1))
    return by_right(jnp.concatenate(lines), fore_z)


def back_plane(modes, plane, target, back_y, back_z):
    along_z = by_right(modes, back_z)
    fields = []
    for duo in range(2):
        both = []
        for f in range(2):
            own = along_z[(2 * duo + f) * KY : (2 * duo + f + 1) * KY]
            both.append(jnp.concatenate([own[:, :N], own[:, N:]]))
        along_y = by_left(back_y, jnp.concatenate(both, axis=1))
        fields += [along_y[:, :N], along_y[:, N:]]
    for part in range(2):
        for block in range(4):
            rows = slice(part * N + block * BLOCK, part * N + (block + 1) * BLOCK)
            for s, piece in enumerate(swap_groups([field[rows] for field in fields])):
                start = ((plane * GROUP + block * 4 + s) * 2 + part) * BLOCK
                target[pl.ds(pl.multiple_of(start, BLOCK), BLOCK), :] = piece


def pack(pieces):
    out = []
    whole = len(pieces) // 3 * 3
    for first in range(0, whole, 3):
        one, two, three = pieces[first : first + 3]
        lane = lax.broadcasted_iota(jnp.int32, one.shape, 1)
        turned = pltpu.roll(two, KZ, 1)
        out.append(jnp.where(lane < KZ, one, turned))
        out.append(jnp.where(lane < 2 * KZ - N, turned, pltpu.roll(three, 2 * KZ - N, 1)))
    return out + list(pieces[whole:])


def unpack(packs, count):
    out = []
    for first in range(0, count // 3 * 2, 2):
        one, two = packs[first : first + 2]
        lane = lax.broadcasted_iota(jnp.int32, one.shape, 1)
        out.append(one)
        out.append(pltpu.roll(jnp.where(lane < 2 * KZ - N, two, one), N - KZ, 1))
        out.append(pltpu.roll(two, 2 * N - 2 * KZ, 1))
    return out + list(packs[count // 3 * 2 :])


def beside(left, right):
    return jnp.concatenate([left, right], axis=1)


def spread_packs(packs, plane, target):
    for owner in range(GROUP):
        for k, values in enumerate(packs):
            start = ((plane * GROUP + owner) * len(packs) + k) * THIN
            target[rows_at(start, THIN), :] = values[owner * THIN : (owner + 1) * THIN]


def gather_packs(source, plane, count):
    packs = []
    for k in range(count):
        starts = [((plane * GROUP + owner) * count + k) * THIN for owner in range(GROUP)]
        packs.append(jnp.concatenate([source[rows_at(at, THIN), :] for at in starts]))
    return packs


def back_along_y(values, plane, target, back_y):
    pieces = []
    for duo in range(2):
        both = []
        for f in (2 * duo, 2 * duo + 1):
            own = values[f * KY : (f + 1) * KY]
            both.append(jnp.concatenate([own[:, :N], own[:, N:]]))
        along = by_left(back_y, beside(*both))
        pieces += [along[:N, :N], along[N:, :N], along[:N, N:], along[N:, N:]]
    spread_packs(pack(pieces), plane, target)


def back_along_z(source, plane, spectral, back_z):
    pieces = unpack(gather_packs(source, plane, SYNTH_PACKS), 8)
    lines = [beside(pieces[2 * f], pieces[2 * f + 1]) for f in range(4)]
    along = by_right(jnp.concatenate(lines), back_z)
    for owner in range(GROUP):
        for f in range(4):
            rows = slice(f * N + owner * THIN, f * N + (owner + 1) * THIN)
            for c in range(2):
                start = ((plane * GROUP + owner) * 2 + c) * PITCH + f * THIN
                spectral[pl.ds(start, THIN), :] = along[rows, c * N : (c + 1) * N]


def fore_along_z(spectral, plane, target, fore_z):
    pieces = []
    for ref in spectral:
        lines = []
        for owner in range(GROUP):
            start = (plane * GROUP + owner) * 2 * PITCH
            both = [ref[pl.ds(start + c * PITCH, BLOCK), :] for c in range(2)]
            lines.append(beside(*both))
        along = by_right(jnp.concatenate(lines), fore_z)
        for f in range(4):
            for c in range(2):
                pieces.append(
                    jnp.concatenate(
                        [
                            along[
                                owner * BLOCK + f * THIN : owner * BLOCK + (f + 1) * THIN,
                                c * N : (c + 1) * N,
                            ]
                            for owner in range(GROUP)
                        ]
                    )
                )
    spread_packs(pack(pieces), plane, target)


def fore_along_y(source, plane, modes, fore_y):
    pieces = unpack(gather_packs(source, plane, PRODUCT_PACKS), 16)
    for duo in range(4):
        both = [
            jnp.concatenate([pieces[2 * f], pieces[2 * f + 1]])
            for f in (2 * duo, 2 * duo + 1)
        ]
        along = by_left(fore_y, beside(*both))
        ref = modes[duo // 2]
        for half in range(2):
            rows = slice((duo % 2 * 2 + half) * KY, (duo % 2 * 2 + half + 1) * KY)
            own = along[:, half * N : (half + 1) * N]
            ref[rows, :N] = own[:KY]
            ref[rows, N:] = own[KY:]


def waves_at(plane):
    _, _, _, me = place()
    wave_x = (me + GROUP * plane).astype(jnp.float32)
    wave_y = (lax.broadcasted_iota(jnp.int32, (KY, N), 0) - KMAX).astype(jnp.float32)
    wave_z = (lax.broadcasted_iota(jnp.int32, (KY, N), 1) - KMAX).astype(jnp.float32)
    return wave_x, wave_y, wave_z


def squared(waves):
    wave_x, wave_y, wave_z = waves
    return wave_x * wave_x + wave_y * wave_y + wave_z * wave_z


def project(velocity, waves, inverse):
    wave_x, wave_y, wave_z = waves
    along = (wave_x * velocity[0] + wave_y * velocity[1] + wave_z * velocity[2]) * inverse
    return (
        velocity[0] - wave_x * along,
        velocity[1] - wave_y * along,
        velocity[2] - wave_z * along,
    )


def linear(state, waves, square, inverse):
    pushed = project((coriolis * state[1], -coriolis * state[0], state[3]), waves, inverse)
    return (
        pushed[0] - viscosity * square * state[0],
        pushed[1] - viscosity * square * state[1],
        pushed[2] - viscosity * square * state[2],
        -buoyancy_square * state[2] - diffusivity * square * state[3],
    )


def propagate(state, waves):
    square = squared(waves)
    inverse = 1.0 / jnp.maximum(square, 1.0)
    for half_step in range(2):
        anchor = state
        for order in (4.0, 3.0, 2.0, 1.0):
            rate = linear(state, waves, square, inverse)
            state = tuple(a + (0.5 * time_step / order) * r for a, r in zip(anchor, rate))
    return state


FIRST_ROW = 16
COARSE_ROWS = 8 * SCAN
TILE = 8 * 4
STEP = 4
LINES = 16


def coarse_waves(plane, row0, rows):
    _, _, _, me = place()
    row = lax.broadcasted_iota(jnp.int32, (rows, N), 0) + row0
    lane = lax.broadcasted_iota(jnp.int32, (rows, N), 1) % 64
    wave_x = (me + GROUP * plane).astype(jnp.float32)
    wave_y = (row - KMAX).astype(jnp.float32)
    wave_z = (lane - KMAX).astype(jnp.float32)
    return wave_x, wave_y, wave_z


def coarse_inside(waves):
    wave_x, wave_y, wave_z = waves
    inside = (jnp.abs(wave_y) <= KCO) & (jnp.abs(wave_z) <= KCO)
    return inside & jnp.broadcast_to(wave_x <= KCO, inside.shape)


def packed(ref, plane, f):
    rows = pl.ds(f * KY + FIRST_ROW, COARSE_ROWS)
    lane = lax.broadcasted_iota(jnp.int32, (COARSE_ROWS, N), 1)
    real, imag = ref[plane, rows, :N], ref[plane, rows, N:]
    return jnp.where(lane < 64, real, pltpu.roll(imag, 64, 1))


class Passing:
    def __init__(self, refs):
        self.source, self.target, self.send, self.receive, self.own = refs

    def rows(self, owner, plane):
        slices = lax.axis_size("tm")
        return pl.ds(pl.multiple_of((plane * slices + owner) * TILE, TILE), TILE)

    def remote(self, i, plane, origin):
        tm, py, pz, _ = place()
        slices = lax.axis_size("tm")
        to = (tm + i) % slices
        where = (tm + slices - i) % slices if origin else tm
        return pltpu.make_async_remote_copy(
            src_ref=self.source.at[self.rows(to, plane), :],
            dst_ref=self.target.at[self.rows(where, plane), :],
            send_sem=self.send.at[plane * slices + i],
            recv_sem=self.receive.at[plane * slices + i],
            device_id=(to, py, pz),
            device_id_type=MESH,
        )

    def local(self, plane):
        tm, _, _, _ = place()
        part = self.rows(tm, plane)
        return pltpu.make_async_copy(
            self.source.at[part, :], self.target.at[part, :], self.own.at[plane]
        )


def whole_kernel(
    fields_hbm, fore_x_hbm, back_x_hbm, fore_y_hbm, back_y_hbm, fore_z_hbm, back_z_hbm,
    into4,
    fields, fore_x, back_x, fore_y, back_y, fore_z, back_z,
    load_sem, table_sem,
    out0, into0, send0, receive0, own0,
    out1, into1, send1, receive1, own1,
    out2, into2, send2, receive2, own2,
    out4, send4, receive4, own4,
    synth, first_products, second_products,
    planes, first_modes, second_modes, start, fine, moved, matrix,
    coarse_out, coarse_in, coarse_send, coarse_receive, coarse_own,
    carry_out, carry_in, carry_send, carry_receive, carry_own,
):
    tm, py, pz, me = place()
    slices = lax.axis_size("tm")
    empty = jnp.zeros((2 * BLOCK, N), jnp.float32)
    into1[pl.ds((KMAX + 1) * SYNTH_PACKS * THIN, EMPTY * SYNTH_PACKS * THIN), :] = jnp.zeros(
        (EMPTY * SYNTH_PACKS * THIN, N), jnp.float32
    )
    into4[pl.ds(GRID_ROWS - 2 * BLOCK, 2 * BLOCK), :] = empty
    coarse_in[...] = jnp.zeros_like(coarse_in)
    barrier = pltpu.get_barrier_semaphore()

    def greet(i, carry):
        peer = (tm, (py + i // 4) % 4, (pz + i % 4) % 4)
        pl.semaphore_signal(barrier, inc=1, device_id=peer, device_id_type=MESH)
        return carry

    lax.fori_loop(1, GROUP, greet, 0)

    def greet_slices(i, carry):
        peer = ((tm + i) % slices, py, pz)
        pl.semaphore_signal(barrier, inc=1, device_id=peer, device_id_type=MESH)
        return carry

    lax.fori_loop(1, slices, greet_slices, 0)

    loads = [
        pltpu.make_async_copy(held, ref, table_sem.at[i])
        for i, (held, ref) in enumerate(
            [
                (fore_x_hbm, fore_x),
                (fore_y_hbm, fore_y),
                (fore_z_hbm, fore_z),
                (back_z_hbm, back_z),
                (back_y_hbm, back_y),
                (back_x_hbm, back_x),
            ]
        )
    ]
    loads[0].start()

    def field_load(step):
        lines = pl.ds(pl.multiple_of(step * STEP, STEP), STEP)
        return pltpu.make_async_copy(
            fields_hbm.at[:, lines], fields.at[:, lines], load_sem.at[step]
        )

    def load(step, carry):
        field_load(step).start()
        return carry

    lax.fori_loop(0, BLOCK // STEP, load, 0)
    for copy in loads[1:]:
        copy.start()
    loads[0].wait()

    analysed = Exchange((out0, into0, send0, receive0, own0), True, 2 * BLOCK)
    to_grid = Exchange((out1, into1, send1, receive1, own1), False, SYNTH_PACKS * THIN)
    to_modes = Exchange((out2, into2, send2, receive2, own2), True, PRODUCT_PACKS * THIN)
    final = Exchange((out4, into4, send4, receive4, own4), False, 2 * BLOCK)
    coarse = Passing((coarse_out, coarse_in, coarse_send, coarse_receive, coarse_own))
    back = Passing((carry_out, carry_in, carry_send, carry_receive, carry_own))
    coarse_second = me + GROUP <= KCO

    def has_coarse(plane):
        return me + GROUP * plane <= KCO

    def analyse(step, carry):
        first = step * STEP
        field_load(step).wait()
        for duo in range(STEP // 2):
            rows = [fields[f, first + 2 * duo + y] for y in range(2) for f in range(4)]
            modes = by_turned(fore_x, jnp.concatenate(rows))
            for y in range(2):
                own = modes[:MODE_ROWS, y * N : (y + 1) * N]
                synth[pl.ds(first + 2 * duo + y, MODE_ROWS, stride=PITCH), :] = own
        return carry

    lax.fori_loop(0, BLOCK // STEP, analyse, 0)
    for slot in range(MODE_ROWS):
        out0[pl.ds(slot * BLOCK, BLOCK), :] = synth[pl.ds(slot * PITCH, BLOCK), :]
    pl.semaphore_wait(barrier, GROUP - 1 + slices - 1)
    for plane in range(PLANES):
        analysed.start(plane)
    for copy in loads[1:]:
        copy.wait()

    def first_pass(plane, carry):
        analysed.arrived(plane)

        @pl.when(me + GROUP * plane <= KMAX)
        def _():
            first_modes[...] = fore_plane(into0, plane, planes, fore_y, fore_z)
            waves = waves_at(plane)
            inverse = 1.0 / jnp.maximum(squared(waves), 1.0)
            for part in range(2):
                lanes = slice(part * N, (part + 1) * N)
                state = [first_modes[f * KY : (f + 1) * KY, lanes] for f in range(4)]
                for f, value in enumerate(project(state[:3], waves, inverse) + (state[3],)):
                    start[plane, pl.ds(f * KY, KY), lanes] = value
            back_along_y(start[plane], plane, out1, back_y)
            to_grid.start(plane)

        return carry

    lax.fori_loop(0, PLANES, first_pass, 0)

    def move(plane, carry):
        @pl.when(has_coarse(plane) & (tm > 0))
        def _():
            waves = coarse_waves(plane, FIRST_ROW, COARSE_ROWS)
            before = tuple(packed(start, plane, f) for f in range(4))
            for f, value in enumerate(propagate(before, waves)):
                moved[plane, f] = value

        @pl.when(has_coarse(plane) & (tm == 0))
        def _():
            moved[plane] = jnp.zeros((4, COARSE_ROWS, N), jnp.float32)

        waves = coarse_waves(plane, FIRST_ROW + tm * 8, 8)
        keep = coarse_inside(waves).astype(jnp.float32)
        zero = jnp.zeros((8, N), jnp.float32)
        for f in range(4):
            unit = tuple(zero + (1.0 if g == f else 0.0) for g in range(4))
            for g, value in enumerate(propagate(unit, waves)):
                matrix[plane, g * 4 + f] = keep * value
        return carry

    lax.fori_loop(0, 2, move, 0)

    def gather(plane, carry):
        to_grid.arrived(plane)
        back_along_z(into1, plane, synth, back_z)
        return carry

    lax.fori_loop(0, PLANES, gather, 0)

    def lines(y, carry):
        slots = 2 * PLANES * GROUP

        def modes_at(ref, f):
            return ref.at[pl.ds(y + f * THIN, slots, stride=PITCH), :]

        grid = []
        for f in (0, 2):
            both = beside(modes_at(synth, f)[...], modes_at(synth, f + 1)[...])
            both = by_left_once(back_x, both)
            grid += [both[:, :N], both[:, N:]]
        u, v, w, b = grid
        rest = w * w
        one = [u * u - rest, v * v - rest, u * v, u * w]
        two = [v * w, u * b, v * b, w * b]
        for ref, values in ((first_products, one), (second_products, two)):
            for f in (0, 2):
                both = by_left_once(fore_x, beside(values[f], values[f + 1]))
                modes_at(ref, f)[...] = both[:, :N]
                modes_at(ref, f + 1)[...] = both[:, N:]
        return carry

    lax.fori_loop(0, THIN, lines, 0)

    def scatter(plane, carry):
        fore_along_z((first_products, second_products), plane, out2, fore_z)
        to_modes.start(plane)
        return carry

    lax.fori_loop(0, PLANES, scatter, 0)

    def second_pass(plane, carry):
        to_modes.arrived(plane)

        @pl.when(me + GROUP * plane <= KMAX)
        def _():
            fore_along_y(into2, plane, (first_modes, second_modes), fore_y)
            waves = waves_at(plane)
            wave_x, wave_y, wave_z = waves
            square = squared(waves)
            inverse = 1.0 / jnp.maximum(square, 1.0)
            for part in range(2):
                lanes = slice(part * N, (part + 1) * N)
                other = slice((1 - part) * N, (2 - part) * N)
                sign = 1.0 if part == 0 else -1.0
                xx, yy, xy, xz = (first_modes[f * KY : (f + 1) * KY, other] for f in range(4))
                yz, bx, by, bz = (second_modes[f * KY : (f + 1) * KY, other] for f in range(4))
                state = [start[plane, pl.ds(f * KY, KY), lanes] for f in range(4)]
                change = (
                    sign * (wave_x * xx + wave_y * xy + wave_z * xz),
                    sign * (wave_x * xy + wave_y * yy + wave_z * yz),
                    sign * (wave_x * xz + wave_y * yz),
                )
                lifted = sign * (wave_x * bx + wave_y * by + wave_z * bz)
                pushed = project(
                    (
                        change[0] + coriolis * state[1],
                        change[1] - coriolis * state[0],
                        change[2] + state[3],
                    ),
                    waves,
                    inverse,
                )
                rates = [pushed[f] - viscosity * square * state[f] for f in range(3)]
                rates.append(
                    lifted - buoyancy_square * state[2] - diffusivity * square * state[3]
                )
                for f in range(4):
                    fine[plane, pl.ds(f * KY, KY), lanes] = state[f] + time_step * rates[f]

        @pl.when(has_coarse(plane))
        def _():
            waves = coarse_waves(plane, FIRST_ROW, COARSE_ROWS)
            keep = coarse_inside(waves).astype(jnp.float32)
            for f in range(4):
                here = keep * packed(fine, plane, f) - keep * moved[plane, f]
                for tile in range(SCAN):
                    at = pl.multiple_of((plane * slices + tile) * TILE + f * 8, 8)
                    coarse_out[pl.ds(at, 8), :] = here[tile * 8 : tile * 8 + 8]

            def go(i, carry):
                @pl.when((tm + i) % slices < SCAN)
                def _():
                    coarse.remote(i, plane, False).start()

                return carry

            for i in range(1, slices):
                go(i, 0)

            @pl.when(tm < SCAN)
            def _():
                coarse.local(plane).start()

        @pl.when((plane == 1) & (tm < SCAN))
        def _():
            def wait(which):
                def go(i, carry):
                    coarse.remote(i, which, True).wait_recv()
                    return carry

                for i in range(1, slices):
                    go(i, 0)
                coarse.local(which).wait()

            wait(0)

            @pl.when(coarse_second)
            def _():
                wait(1)

            def rows(n, which, f):
                return pl.ds(pl.multiple_of((which * slices + n) * TILE + f * 8, 8), 8)

            def step(n, state):
                new = []
                for which in range(2):
                    held = state[which * 4 : which * 4 + 4]
                    for g in range(4):
                        value = coarse_in[rows(n, which, g), :]
                        for f in range(4):
                            value = value + matrix[which, g * 4 + f] * held[f]
                        carry_out[rows(n, which, g), :] = value
                        new.append(value)
                return tuple(new)

            lax.fori_loop(0, slices, step, tuple([jnp.zeros((8, N), jnp.float32)] * 8))

            def send(which):
                def go(i, carry):
                    back.remote(i, which, False).start()
                    return carry

                for i in range(1, slices):
                    go(i, 0)
                back.local(which).start()

            send(0)

            @pl.when(coarse_second)
            def _():
                send(1)

        return carry

    lax.fori_loop(0, PLANES, second_pass, 0)

    def last_pass(step, carry):
        plane = PLANES - 1 - step

        @pl.when(me + GROUP * plane <= KMAX)
        def _():
            @pl.when((plane < 2) & has_coarse(plane))
            def _():
                def wait(i, carry):
                    @pl.when((tm + slices - i) % slices < SCAN)
                    def _():
                        back.remote(i, plane, True).wait_recv()

                    return carry

                for i in range(1, slices):
                    wait(i, 0)

                @pl.when(tm < SCAN)
                def _():
                    back.local(plane).wait()

                waves = coarse_waves(plane, FIRST_ROW, COARSE_ROWS)
                lane = lax.broadcasted_iota(jnp.int32, (COARSE_ROWS, N), 1)
                here = coarse_inside(waves) & (lane < 64)
                for f in range(4):
                    tiles = []
                    for tile in range(SCAN):
                        at = pl.multiple_of((plane * slices + tile) * TILE + f * 8, 8)
                        tiles.append(carry_in[pl.ds(at, 8), :])
                    value = jnp.concatenate(tiles)
                    rows = pl.ds(f * KY + FIRST_ROW, COARSE_ROWS)
                    fine[plane, rows, :N] = jnp.where(here, value, fine[plane, rows, :N])
                    fine[plane, rows, N:] = jnp.where(
                        here, pltpu.roll(value, 64, 1), fine[plane, rows, N:]
                    )

            back_plane(fine[plane], plane, out4, back_y, back_z)
            final.start(plane)

        return carry

    lax.fori_loop(0, PLANES, last_pass, 0)

    def done(plane, carry):
        analysed.sent(plane)
        to_grid.sent(plane)
        to_modes.sent(plane)
        final.sent(plane)
        final.arrived(plane)
        return carry

    lax.fori_loop(0, PLANES, done, 0)

    def passed(q, carry):
        plane, i = q // slices, q % slices

        @pl.when((i > 0) & has_coarse(plane))
        def _():
            @pl.when((tm + i) % slices < SCAN)
            def _():
                coarse.remote(i, plane, False).wait_send()

            @pl.when(tm < SCAN)
            def _():
                back.remote(i, plane, False).wait_send()

        return carry

    lax.fori_loop(0, 2 * slices, passed, 0)


def lines_kernel(modes, back_x, out, held):
    @pl.when(pl.program_id(0) == 0)
    def _():
        for slot in range(MODE_ROWS):
            held[pl.ds(slot * PITCH, BLOCK), :] = modes[pl.ds(slot * BLOCK, BLOCK), :]

    grid = load_fields_x(held, back_x, pl.program_id(0) * LINES, LINES)
    for y in range(LINES):
        for f in range(4):
            at = y * N + f * BLOCK
            out[f, y] = grid[at : at + BLOCK]


def on_device(state_old):
    slices = lax.axis_size("tm")
    fields = state_old[0]
    held = [jnp.asarray(table) for table in tables()]
    inner = held[:-1]
    inputs = [pltpu.with_memory_space_constraint(a, pltpu.HBM) for a in [fields] + inner]
    half = pltpu.VMEM((4 * KY, 2 * N), jnp.float32)
    modes = pltpu.VMEM((PLANES, 4 * KY, 2 * N), jnp.float32)
    passing = [
        pltpu.VMEM((2 * slices * TILE, N), jnp.float32),
        pltpu.VMEM((2 * slices * TILE, N), jnp.float32),
        pltpu.SemaphoreType.DMA((2 * slices,)),
        pltpu.SemaphoreType.DMA((2 * slices,)),
        pltpu.SemaphoreType.DMA((2,)),
    ]
    last = exchange_scratch(PLANE_ROWS, GRID_ROWS)
    synth_rows = PLANES * GROUP * SYNTH_PACKS * THIN
    product_rows = PLANES * GROUP * PRODUCT_PACKS * THIN
    spectral = pltpu.VMEM((SPECTRAL_ROWS, N), jnp.float32)
    arrived = pl.pallas_call(
        whole_kernel,
        name="whole",
        out_shape=jax.ShapeDtypeStruct((GRID_ROWS, N), jnp.float32),
        in_specs=[pl.BlockSpec(memory_space=pltpu.HBM)] * len(inputs),
        out_specs=pl.BlockSpec(memory_space=pltpu.VMEM),
        scratch_shapes=[pltpu.VMEM(a.shape, a.dtype) for a in inputs]
        + [
            pltpu.SemaphoreType.DMA((BLOCK // STEP,)),
            pltpu.SemaphoreType.DMA((len(inner),)),
        ]
        + exchange_scratch(GRID_ROWS, PLANE_ROWS)
        + exchange_scratch(synth_rows, synth_rows)
        + exchange_scratch(product_rows, product_rows)
        + [last[0]]
        + last[2:]
        + [spectral, spectral, spectral]
        + [
            pltpu.VMEM((2, 2 * N, 2 * N), jnp.float32),
            half,
            half,
            modes,
            modes,
            pltpu.VMEM((2, 4, COARSE_ROWS, N), jnp.float32),
            pltpu.VMEM((2, 16, 8, N), jnp.float32),
        ]
        + passing
        + passing,
        compiler_params=pltpu.CompilerParams(
            collective_id=0, has_side_effects=True, vmem_limit_bytes=VMEM_BYTES
        ),
    )(*inputs)
    result = pl.pallas_call(
        lines_kernel,
        name="lines",
        grid=(BLOCK // LINES,),
        out_shape=jax.ShapeDtypeStruct(fields.shape, jnp.float32),
        in_specs=[pl.BlockSpec(memory_space=pltpu.VMEM)] * 2,
        scratch_shapes=[pltpu.VMEM((MODE_ROWS * PITCH, N), jnp.float32)],
        out_specs=pl.BlockSpec((4, LINES, BLOCK, N), lambda i: (0, i, 0, 0)),
        compiler_params=pltpu.CompilerParams(vmem_limit_bytes=16 << 20),
    )(arrived, held[-1])
    return result[None]


def solution(mesh):
    return jax.shard_map(
        on_device,
        mesh=mesh,
        in_specs=(P("tm", None, "py", "pz", None),),
        out_specs=P("tm", None, "py", "pz", None),
        check_vma=False,
    )
```
